32 devices in a mesh: clip: 2 (over x), frame: 4 (over z), tile: 4 (over y, core).
Axes of the slice: x: 2, y: 2, z: 4, core: 2. Of those that a mesh axis runs over, the one named last changes fastest.
Arguments:
- queries: bfloat16 [8, 8, 64, 1536], P(('clip', 'frame'), None, 'tile'), parts along dimension 0, may hold values from -5 to 5
- keys: bfloat16 [8, 8, 64, 1536], P(('clip', 'frame'), None, 'tile'), parts along dimension 0, may hold values from -5 to 5
- values: bfloat16 [8, 8, 64, 1536], P(('clip', 'frame'), None, 'tile'), parts along dimension 0, may hold values from -6 to 6
- grad_out: bfloat16 [8, 8, 64, 1536], P(('clip', 'frame'), None, 'tile'), parts along dimension 0, may hold values from -6 to 6
- window: int32 [18, 3], replicated, may hold values from -1 to 1, as said below
Outputs:
- key_grad: bfloat16 [8, 8, 64, 1536], P(('clip', 'frame'), None, 'tile'), parts along dimension 0
- value_grad: bfloat16 [8, 8, 64, 1536], P(('clip', 'frame'), None, 'tile'), parts along dimension 0
The draws below stay inside these ranges and needn't reach their ends.
There are 2 independent parts, one for each index of `clip`. The reference program is written for one: setup_inputs(seed, part) draws one part's arguments, and reference() takes and returns one part's arrays. A program takes and returns all parts, laid end to end along the dimension named above; an argument that names none is the same for every part. Nothing has to cross between parts.
Inputs may be any that keep to these rules, and one draw needn't show every extreme that they name: For each of the nine pairs of frame and column tile offsets the window lists exactly two of the three row offsets; it always lists (0, 0, 0); its rows are distinct.
All inputs are finite; a program needn't handle non-finite values.
Results may differ from the reference program's by a relative error of at most 0.0065.
Values may be sent and summed in bfloat16 or wider, within the bound.
No kernel may reach another device: no remote copies, remote signals or barrier semaphores. Data moves between devices by JAX's collectives and lax.ppermute only.
A program may use at most 64 MiB of HBM per device.

```python
import jax
import jax.numpy as jnp
from jax import lax

HEADS = 12
HD = 128
TT = 1
TH = 4
TW = 8
FT = 1
HEIGHT = 8
WSTRIP = 16
FRAMES = 4
WIDTH = 64
N_FRAME = 4
N_TILE = 4


def draw_pair(key):
    shape = (FRAMES, HEIGHT, WIDTH, HEADS * HD)
    query_draw = jax.random.normal(jax.random.fold_in(key, 11), shape, jnp.float32)
    key_draw = jax.random.normal(jax.random.fold_in(key, 12), shape, jnp.float32)
    return (jnp.clip(query_draw, -5.0, 5.0), jnp.clip(key_draw, -5.0, 5.0))


def draw_queries(key, part):
    return draw_pair(key)[0].astype(jnp.bfloat16)


def draw_keys(key, part):
    return draw_pair(key)[1].astype(jnp.bfloat16)


def draw_window(key, part):
    dropped = jax.random.randint(jax.random.fold_in(key, 21), (9,), 0, 3)
    centre = jax.random.randint(jax.random.fold_in(key, 22), (), 0, 2) * 2
    pair_ids = jnp.arange(9, dtype=jnp.int32)
    dropped = jnp.where(pair_ids == 4, centre, dropped)
    time_off = pair_ids // 3 - 1
    wide_off = pair_ids % 3 - 1
    first_high = jnp.where(dropped == 0, 1, 0) - 1
    second_high = jnp.where(dropped == 2, 1, 2) - 1
    rows_a = jnp.stack([time_off, first_high, wide_off], axis=1)
    rows_b = jnp.stack([time_off, second_high, wide_off], axis=1)
    return jnp.concatenate([rows_a, rows_b], axis=0).astype(jnp.int32)


def levels(rng, dims, pieces, smallest, top_value):
    gain, own = 1.0, jax.random.fold_in(rng, 6)
    for position, blocks in pieces:
        draws = jnp.exp(jax.random.uniform(jax.random.fold_in(own, position), (blocks,), jnp.float32, smallest / len(pieces), top_value / len(pieces)))
        gain = gain * jnp.repeat(draws, dims[position] // blocks).reshape([-1 if axis == position else 1 for axis in range(len(dims))])
    return gain


def bell_draw(stream_key, extent, scale, most, shards=(), kind=jnp.bfloat16):
    entries = jax.random.normal(stream_key, extent, jnp.float32) * scale
    if len(shards) > 0:
        entries = levels(stream_key, extent, shards, -0.22, 0.18) * entries
    return jnp.clip(entries, min=-most, max=most).astype(kind)


def setup_inputs(seed: int = 0, part: int = 0) -> dict:
    key_list = jax.random.split(jax.random.key(seed), 6)
    part_keys = jax.random.split(jax.random.fold_in(key_list[5], part), 6)
    queries = draw_queries(jax.random.fold_in(jax.random.fold_in(key_list[5], part), 71), part)
    keys = draw_keys(jax.random.fold_in(jax.random.fold_in(key_list[5], part), 71), part)
    values = bell_draw(part_keys[2], (FRAMES, HEIGHT, WIDTH, HEADS * HD), 1.0, 6.0, ((0, 4), (2, 4)))
    grad_out = bell_draw(part_keys[3], (FRAMES, HEIGHT, WIDTH, HEADS * HD), 1.0, 6.0, ((0, 4), (2, 4)))
    window = draw_window(jax.random.fold_in(key_list[5], 71), part)
    return {"queries": queries, "keys": keys, "values": values, "grad_out": grad_out, "window": window}


def window_mask(window, frame_pos, frame_count, strip_pos, strip_count, time_tiles, height_tiles, strip_tiles):
    q_time = jnp.arange(time_tiles, dtype=jnp.int32)
    k_time = jnp.arange(time_tiles + 2, dtype=jnp.int32)
    q_high = jnp.arange(height_tiles, dtype=jnp.int32)
    q_wide = jnp.arange(strip_tiles, dtype=jnp.int32)
    k_wide = jnp.arange(strip_tiles + 2, dtype=jnp.int32)
    off_time = k_time[None, :] - q_time[:, None] - 1
    off_high = q_high[None, :] - q_high[:, None]
    off_wide = k_wide[None, :] - q_wide[:, None] - 1
    tile_codes = ((off_time[:, None, None, :, None, None] + 1) * 9
                  + (off_high[None, :, None, None, :, None] + 1) * 3
                  + (off_wide[None, None, :, None, None, :] + 1))
    is_near = ((jnp.abs(off_time) <= 1)[:, None, None, :, None, None]
               & (jnp.abs(off_high) <= 1)[None, :, None, None, :, None]
               & (jnp.abs(off_wide) <= 1)[None, None, :, None, None, :])
    listed_codes = (window[:, 0] + 1) * 9 + (window[:, 1] + 1) * 3 + (window[:, 2] + 1)
    code_range = jnp.arange(27, dtype=jnp.int32)
    chosen = jnp.any(listed_codes[:, None] == code_range[None, :], axis=0)
    allowed = jnp.any((tile_codes[..., None] == code_range) & chosen, axis=-1) & is_near
    glob_time = frame_pos * time_tiles + k_time - 1
    glob_wide = strip_pos * strip_tiles + k_wide - 1
    inside_time = (glob_time >= 0) & (glob_time < frame_count * time_tiles)
    inside_wide = (glob_wide >= 0) & (glob_wide < strip_count * strip_tiles)
    allowed = allowed & inside_time[None, None, None, :, None, None] & inside_wide[None, None, None, None, None, :]
    token_mask = jnp.broadcast_to(
        allowed[:, None, :, None, :, None, :, None, :, None, :, None],
        (time_tiles, TT, height_tiles, TH, strip_tiles, TW, time_tiles + 2, TT, height_tiles, TH, strip_tiles + 2, TW))
    row_count = time_tiles * TT * height_tiles * TH * strip_tiles * TW
    return token_mask.reshape(row_count, -1)


def rounded(array):
    return lax.optimization_barrier(array.astype(jnp.bfloat16)).astype(jnp.float32)


def group_grads(query_g, key_g, value_g, grad_g, token_mask):
    scale_qk = HD ** -0.5
    high = lax.Precision.HIGHEST
    query_f = query_g.astype(jnp.float32)
    key_f = key_g.astype(jnp.float32)
    value_f = value_g.astype(jnp.float32)
    grad_f = grad_g.astype(jnp.float32)
    scores = jnp.einsum("qhd,khd->hqk", query_f, key_f, precision=high) * scale_qk
    scores = jnp.where(token_mask[None], scores, -jnp.inf)
    top_score = jnp.max(scores, axis=-1, keepdims=True)
    exp_scores = jnp.exp(scores - top_score)
    attn_probs = exp_scores / jnp.sum(exp_scores, axis=-1, keepdims=True)
    probs_low = rounded(attn_probs)
    attended = jnp.einsum("hqk,khd->qhd", probs_low, value_f, precision=high)
    row_delta = jnp.sum(grad_f * attended, axis=-1)
    grad_probs = jnp.einsum("qhd,khd->hqk", grad_f, value_f, precision=high)
    grad_scores = rounded(attn_probs * (grad_probs - row_delta.T[:, :, None]) * scale_qk)
    value_part = jnp.einsum("hqk,qhd->khd", probs_low, grad_f, precision=high)
    key_part = jnp.einsum("hqk,qhd->khd", grad_scores, query_f, precision=high)
    return key_part, value_part


def reference(queries, keys, values, grad_out, window):
    chans = HEADS * HD
    stacked = jnp.stack([keys, values])
    padded = jnp.pad(stacked, ((0, 0), (TT, TT), (0, 0), (TW, TW), (0, 0)))
    row_count = FT * HEIGHT * WSTRIP
    ext_count = (FT + 2 * TT) * HEIGHT * (WSTRIP + 2 * TW)
    zero_idx = jnp.zeros((), jnp.int32)

    def visit(totals, block_idx):
        frame_pos = (block_idx // N_TILE).astype(jnp.int32)
        strip_pos = (block_idx % N_TILE).astype(jnp.int32)
        first_frame = (frame_pos * FT).astype(jnp.int32)
        first_col = (strip_pos * WSTRIP).astype(jnp.int32)
        query_blk = lax.dynamic_slice(queries, (first_frame, zero_idx, first_col, zero_idx), (FT, HEIGHT, WSTRIP, chans))
        grad_blk = lax.dynamic_slice(grad_out, (first_frame, zero_idx, first_col, zero_idx), (FT, HEIGHT, WSTRIP, chans))
        corner = (zero_idx, first_frame, zero_idx, first_col, zero_idx)
        beside_all = lax.dynamic_slice(padded, corner, (2, FT + 2 * TT, HEIGHT, WSTRIP + 2 * TW, chans))
        token_mask = window_mask(window, frame_pos, N_FRAME, strip_pos, N_TILE, FT // TT, HEIGHT // TH, WSTRIP // TW)
        key_part, value_part = group_grads(
            query_blk.reshape(row_count, HEADS, HD),
            beside_all[0].reshape(ext_count, HEADS, HD),
            beside_all[1].reshape(ext_count, HEADS, HD),
            grad_blk.reshape(row_count, HEADS, HD),
            token_mask)
        update = jnp.stack([key_part, value_part]).reshape(2, FT + 2 * TT, HEIGHT, WSTRIP + 2 * TW, chans)
        current = lax.dynamic_slice(totals, corner, update.shape)
        return lax.dynamic_update_slice(totals, current + update, corner), None

    start_totals = jnp.zeros(padded.shape, jnp.float32)
    totals, unused = lax.scan(visit, start_totals, jnp.arange(N_FRAME * N_TILE, dtype=jnp.int32))
    interior = totals[:, TT:TT + FRAMES, :, TW:TW + WIDTH]
    return interior[0].astype(jnp.bfloat16), interior[1].astype(jnp.bfloat16)
```

```python
import math

import jax
import jax.numpy as jnp
from jax import lax
from jax.experimental import pallas as pl
from jax.experimental.pallas import tpu as pltpu
from jax.sharding import PartitionSpec as P

HD = 128
TH = 4
TW = 8
STEP_HEADS = 3
NEG = -1e30
FLOOR = -1e29
SCALE = HD ** (-0.5)
SCALE2 = SCALE * math.log2(math.e)


def pair_lists(count):
    even = [(i, i + 1) for i in range(0, count - 1, 2)]
    odd = [(i, i + 1) for i in range(1, count - 1, 2)]
    far_a = [(i, i + 2) for i in range(count - 2) if i % 4 in (0, 1)]
    far_b = [(i, i + 2) for i in range(count - 2) if i % 4 in (2, 3)]
    return [pairs + [(j, i) for i, j in pairs] for pairs in (even, odd, far_a, far_b)]


def swap(value, axis, pairs):
    return lax.ppermute(value, axis, pairs)


def bit_table(window_ref):
    bits = jnp.int32(0)
    for i in range(window_ref.shape[0]):
        code = (window_ref[i, 0] + 1) * 9 + (window_ref[i, 1] + 1) * 3 + (window_ref[i, 2] + 1)
        bits = bits | jnp.left_shift(jnp.int32(1), code)
    return bits


def position_facts(place_ref, frame_count, strip_count):
    frame = place_ref[0]
    strip = place_ref[1]
    step_f = 1 - 2 * (frame & 1)
    step_s = 1 - 2 * (strip & 1)
    return (
        frame,
        step_f,
        step_s,
        ((frame + step_f >= 0) & (frame + step_f < frame_count)).astype(jnp.int32),
        ((frame - step_f >= 0) & (frame - step_f < frame_count)).astype(jnp.int32),
        ((strip + step_s >= 0) & (strip + step_s < strip_count)).astype(jnp.int32),
        ((strip - step_s >= 0) & (strip - step_s < strip_count)).astype(jnp.int32),
    )


def fill_bias(bias_ref, window_ref, place_ref, frame_count, strip_count, height, strip):
    bits = bit_table(window_ref)
    _, step_f, step_s, has_fa, has_fb, has_sa, has_sb = position_facts(
        place_ref, frame_count, strip_count
    )
    rows = height * strip
    half = height * TW
    tiles = strip // TW
    col_a = jnp.where(step_s > 0, tiles, -1)
    col_b = jnp.where(step_s > 0, -1, tiles)
    for slot, (off_time, has_f) in enumerate(((0, 1), (-step_f, has_fa), (step_f, has_fb))):
        start = 0
        for length, wide, k_col, has_s in (
            (rows, strip, None, 1),
            (half, TW, col_a, has_sa),
            (half, TW, col_b, has_sb),
        ):
            key_idx = lax.broadcasted_iota(jnp.int32, (length, rows), 0)
            query_idx = lax.broadcasted_iota(jnp.int32, (length, rows), 1)
            off_high = key_idx // (wide * TH) - query_idx // (strip * TH)
            k_wide = (key_idx % wide) // TW if k_col is None else k_col
            off_wide = k_wide - (query_idx % strip) // TW
            near = (jnp.abs(off_wide) <= 1) & (jnp.abs(off_high) <= 1)
            code = (off_time + 1) * 9 + (off_high + 1) * 3 + (off_wide + 1)
            listed = jnp.right_shift(bits, jnp.where(near, code, 0)) & 1
            flag = jnp.where(near, listed, 0) * (has_f * has_s)
            bias_ref[start : start + length, slot * rows : (slot + 1) * rows] = jnp.where(
                flag == 1, jnp.float32(0), jnp.float32(NEG)
            )
            start += length


def head_rows(ref, head):
    block = ref[0, :, :, head * HD : (head + 1) * HD]
    return block.reshape(-1, HD)


def load_queries(refs, head):
    return jnp.concatenate([head_rows(ref, head) for ref in refs], axis=0)


def load_keys(own_ref, a_ref, b_ref, which, head):
    lanes = slice(head * HD, (head + 1) * HD)
    return jnp.concatenate(
        [head_rows(own_ref, head), a_ref[which, :, lanes], b_ref[which, :, lanes]], axis=0
    )


def dot_nt(a, b):
    return lax.dot_general(a, b, (((1,), (1,)), ((), ())), preferred_element_type=jnp.float32)


def stats_kernel(frame_count, strip_count, height, strip, *refs):
    (window_ref, place_ref, q0, qa, qb, g0, ga, gb, k0, v0, ha, hb, own_out, a_out, b_out, c_out, d_out, bias_ref) = refs
    rows = height * strip

    @pl.when(pl.program_id(0) == 0)
    def _():
        fill_bias(bias_ref, window_ref, place_ref, frame_count, strip_count, height, strip)

    far_slot_a = ((place_ref[0] & 3) == 0) | ((place_ref[0] & 3) == 3)
    for head in range(STEP_HEADS):
        query = load_queries((q0, qa, qb), head)
        grad = load_queries((g0, ga, gb), head)
        key = load_keys(k0, ha, hb, 0, head)
        value = load_keys(v0, ha, hb, 1, head)
        scores = dot_nt(key, query) * SCALE2 + bias_ref[...]
        grad_probs = dot_nt(value, grad)
        top = jnp.max(scores, axis=0, keepdims=True)
        expo = jnp.exp2(scores - top)
        total = jnp.sum(expo, axis=0, keepdims=True)
        delta = jnp.sum(expo * grad_probs, axis=0, keepdims=True) / total
        lse = top + jnp.log2(total)
        parts = [
            jnp.concatenate([lse[:, i * rows : (i + 1) * rows], delta[:, i * rows : (i + 1) * rows]], axis=0)
            for i in range(3)
        ]
        own_out[head] = jnp.concatenate(parts, axis=0)
        a_out[head] = jnp.concatenate([parts[0], parts[1]], axis=0)
        b_out[head] = jnp.concatenate([parts[0], parts[2]], axis=0)
        c_out[head] = jnp.where(far_slot_a, parts[1], parts[2])
        d_out[head] = jnp.where(far_slot_a, parts[2], parts[1])


def merge(parts):
    top = parts[0][0]
    for lse, _ in parts[1:]:
        top = jnp.maximum(top, lse)
    weight_sum = jnp.zeros_like(top)
    delta_sum = jnp.zeros_like(top)
    for lse, delta in parts:
        weight = jnp.exp2(lse - top)
        weight_sum = weight_sum + weight
        delta_sum = delta_sum + weight * delta
    return jnp.maximum(top + jnp.log2(weight_sum), FLOOR), delta_sum / weight_sum


def grads_kernel(frame_count, strip_count, height, strip, *refs):
    (window_ref, place_ref, q0, qa, qb, g0, ga, gb, k0, v0, ha, hb, own_st, a_st, b_st, c_st, d_st, dk_out, dv_out, ra_out, rb_out, bias_ref) = refs
    rows = height * strip
    half = height * TW

    @pl.when(pl.program_id(0) == 0)
    def _():
        fill_bias(bias_ref, window_ref, place_ref, frame_count, strip_count, height, strip)

    frame, step_f, _, has_fa, has_fb, _, _ = position_facts(place_ref, frame_count, strip_count)
    beyond_a = frame + 2 * step_f
    beyond_b = frame - 2 * step_f
    has_ba = (beyond_a >= 0) & (beyond_a < frame_count)
    has_bb = (beyond_b >= 0) & (beyond_b < frame_count)
    far_slot_a = ((frame & 3) == 0) | ((frame & 3) == 3)

    def part(block, row, exists):
        lse = block[row : row + 1, :]
        return (lse if exists is None else jnp.where(exists, lse, NEG), block[row + 1 : row + 2, :])

    for head in range(STEP_HEADS):
        lanes = slice(head * HD, (head + 1) * HD)
        own, from_a, from_b, from_c, from_d = (r[head] for r in (own_st, a_st, b_st, c_st, d_st))
        far_a = jnp.where(far_slot_a, from_c, from_d)
        far_b = jnp.where(far_slot_a, from_d, from_c)
        merged = [
            merge([part(own, 0, None), part(from_a, 2, has_fa == 1), part(from_b, 2, has_fb == 1)]),
            merge([part(own, 2, None), part(from_a, 0, has_fa == 1), part(far_a, 0, has_ba)]),
            merge([part(own, 4, None), part(from_b, 0, has_fb == 1), part(far_b, 0, has_bb)]),
        ]
        lse = jnp.concatenate([m[0] for m in merged], axis=1)
        delta = jnp.concatenate([m[1] for m in merged], axis=1)
        query = load_queries((q0, qa, qb), head)
        grad = load_queries((g0, ga, gb), head)
        key = load_keys(k0, ha, hb, 0, head)
        value = load_keys(v0, ha, hb, 1, head)
        scores = dot_nt(key, query) * SCALE2 + bias_ref[...]
        probs = jnp.exp2(scores - lse)
        grad_probs = dot_nt(value, grad)
        grad_scores = (probs * (grad_probs - delta) * SCALE).astype(jnp.bfloat16)
        value_part = jnp.dot(probs.astype(jnp.bfloat16), grad, preferred_element_type=jnp.float32)
        key_part = jnp.dot(grad_scores, query, preferred_element_type=jnp.float32)
        dk_out[:, lanes] = key_part[:rows]
        dv_out[:, lanes] = value_part[:rows]
        for out, lo in ((ra_out, rows), (rb_out, rows + half)):
            out[0, :, lanes] = key_part[lo : lo + half].astype(jnp.bfloat16)
            out[1, :, lanes] = value_part[lo : lo + half].astype(jnp.bfloat16)


def finish_kernel(height, strip, place_ref, dk, dv, ra, rb, dk_out, dv_out):
    even = (place_ref[1] & 1) == 0
    for which, (part, out) in enumerate(((dk, dk_out), (dv, dv_out))):
        from_a = ra[which].astype(jnp.float32).reshape(height, TW, -1)
        from_b = rb[which].astype(jnp.float32).reshape(height, TW, -1)
        full = part[...].reshape(height, strip, -1)
        left = full[:, :TW] + jnp.where(even, from_b, from_a)
        right = full[:, TW:] + jnp.where(even, from_a, from_b)
        out[0] = jnp.concatenate([left, right], axis=1).astype(jnp.bfloat16)


def on_device(queries, keys, values, grad_out, window):
    _, height, strip, chans = queries.shape
    heads = chans // HD
    rows = height * strip
    half = height * TW
    frame_count = lax.axis_size("frame")
    strip_count = lax.axis_size("tile")
    frame_even, frame_odd, far_c, far_d = pair_lists(frame_count)
    tile_even, tile_odd, _, _ = pair_lists(strip_count)
    frame_pos = lax.axis_index("frame")
    strip_pos = lax.axis_index("tile")
    place = jnp.stack([frame_pos, strip_pos]).astype(jnp.int32)

    qa = swap(queries, "frame", frame_even)
    qb = swap(queries, "frame", frame_odd)
    ga = swap(grad_out, "frame", frame_even)
    gb = swap(grad_out, "frame", frame_odd)

    even = (strip_pos & 1) == 0
    start_a = jnp.where(even, strip - TW, 0)
    start_b = jnp.where(even, 0, strip - TW)

    def edge(start):
        cut = [lax.dynamic_slice_in_dim(x[0], start, TW, axis=1).reshape(half, chans) for x in (keys, values)]
        return jnp.stack(cut)

    ha = swap(edge(start_a), "tile", tile_even)
    hb = swap(edge(start_b), "tile", tile_odd)

    steps = heads // STEP_HEADS
    lanes = STEP_HEADS * HD
    wide_spec = pl.BlockSpec((1, height, strip, lanes), lambda i: (0, 0, 0, i))
    halo_spec = pl.BlockSpec((2, half, lanes), lambda i: (0, 0, i))
    flat_spec = pl.BlockSpec((rows, lanes), lambda i: (0, i))
    smem = pl.BlockSpec(memory_space=pltpu.SMEM)

    def stat_spec(count):
        return pl.BlockSpec((STEP_HEADS, count, rows), lambda i: (i, 0, 0))

    def stat_shape(count):
        return jax.ShapeDtypeStruct((heads, count, rows), jnp.float32)

    data = (queries, qa, qb, grad_out, ga, gb, keys, values, ha, hb)
    data_specs = [smem, smem] + [wide_spec] * 8 + [halo_spec] * 2
    sizes = (6, 4, 4, 2, 2)
    bias = pltpu.VMEM((rows + 2 * half, 3 * rows), jnp.float32)
    own_st, a_st, b_st, c_st, d_st = pl.pallas_call(
        lambda *refs: stats_kernel(frame_count, strip_count, height, strip, *refs),
        name="stats",
        grid=(steps,),
        in_specs=data_specs,
        out_specs=[stat_spec(n) for n in sizes],
        out_shape=[stat_shape(n) for n in sizes],
        scratch_shapes=[bias],
    )(window, place, *data)

    a_st = swap(a_st, "frame", frame_even)
    b_st = swap(b_st, "frame", frame_odd)
    if far_c:
        c_st = swap(c_st, "frame", far_c)
    if far_d:
        d_st = swap(d_st, "frame", far_d)

    dk, dv, ra, rb = pl.pallas_call(
        lambda *refs: grads_kernel(frame_count, strip_count, height, strip, *refs),
        name="grads",
        grid=(steps,),
        in_specs=data_specs + [stat_spec(n) for n in sizes],
        out_specs=[flat_spec, flat_spec, halo_spec, halo_spec],
        out_shape=[jax.ShapeDtypeStruct((rows, chans), jnp.float32)] * 2
        + [jax.ShapeDtypeStruct((2, half, chans), jnp.bfloat16)] * 2,
        scratch_shapes=[bias],
    )(window, place, *data, own_st, a_st, b_st, c_st, d_st)

    ra = swap(ra, "tile", tile_even)
    rb = swap(rb, "tile", tile_odd)
    return pl.pallas_call(
        lambda *refs: finish_kernel(height, strip, *refs),
        name="finish",
        grid=(steps,),
        in_specs=[smem, flat_spec, flat_spec, halo_spec, halo_spec],
        out_specs=[wide_spec, wide_spec],
        out_shape=[jax.ShapeDtypeStruct(keys.shape, jnp.bfloat16)] * 2,
    )(place, dk, dv, ra, rb)


def solution(mesh):
    spec = P(("clip", "frame"), None, "tile", None)
    return jax.shard_map(
        on_device,
        mesh=mesh,
        in_specs=(spec, spec, spec, spec, P()),
        out_specs=(spec, spec),
        check_vma=False,
    )
```

```python
import math

import jax
import jax.numpy as jnp
from jax import lax
from jax.experimental import pallas as pl
from jax.experimental.pallas import tpu as pltpu
from jax.sharding import PartitionSpec as P

HD = 128
TH = 4
TW = 8
FINISH_STEPS = 4
KERNEL_VMEM = 16 << 20
NEG = -1e30
FLOOR = -1e29
SCALE = HD ** (-0.5)
SCALE2 = SCALE * math.log2(math.e)


def pair_lists(count):
    even = [(i, i + 1) for i in range(0, count - 1, 2)]
    odd = [(i, i + 1) for i in range(1, count - 1, 2)]
    far_a = [(i, i + 2) for i in range(count - 2) if i % 4 in (0, 1)]
    far_b = [(i, i + 2) for i in range(count - 2) if i % 4 in (2, 3)]
    return [pairs + [(j, i) for i, j in pairs] for pairs in (even, odd, far_a, far_b)]


def swap(value, axis, pairs):
    return lax.ppermute(value, axis, pairs)


def bit_table(window_ref):
    bits = jnp.int32(0)
    for i in range(window_ref.shape[0]):
        code = (window_ref[i, 0] + 1) * 9 + (window_ref[i, 1] + 1) * 3 + (window_ref[i, 2] + 1)
        bits = bits | jnp.left_shift(jnp.int32(1), code)
    return bits


def position_facts(place_ref, frame_count, strip_count):
    frame = place_ref[0]
    strip = place_ref[1]
    step_f = 1 - 2 * (frame & 1)
    step_s = 1 - 2 * (strip & 1)
    return (
        frame,
        step_f,
        step_s,
        ((frame + step_f >= 0) & (frame + step_f < frame_count)).astype(jnp.int32),
        ((frame - step_f >= 0) & (frame - step_f < frame_count)).astype(jnp.int32),
        ((strip + step_s >= 0) & (strip + step_s < strip_count)).astype(jnp.int32),
        ((strip - step_s >= 0) & (strip - step_s < strip_count)).astype(jnp.int32),
    )


def fill_bias(bias_ref, slots, window_ref, place_ref, frame_count, strip_count, height, strip):
    bits = bit_table(window_ref)
    _, step_f, step_s, has_fa, has_fb, has_sa, has_sb = position_facts(
        place_ref, frame_count, strip_count
    )
    rows = height * strip
    half = height * TW
    tiles = strip // TW
    col_a = jnp.where(step_s > 0, tiles, -1)
    col_b = jnp.where(step_s > 0, -1, tiles)
    frames = ((0, 1), (-step_f, has_fa), (step_f, has_fb))
    for place, slot in enumerate(slots):
        off_time, has_f = frames[slot]
        start = 0
        for length, wide, k_col, has_s in (
            (rows, strip, None, 1),
            (half, TW, col_a, has_sa),
            (half, TW, col_b, has_sb),
        ):
            key_idx = lax.broadcasted_iota(jnp.int32, (length, rows), 0)
            query_idx = lax.broadcasted_iota(jnp.int32, (length, rows), 1)
            off_high = key_idx // (wide * TH) - query_idx // (strip * TH)
            k_wide = (key_idx % wide) // TW if k_col is None else k_col
            off_wide = k_wide - (query_idx % strip) // TW
            near = (jnp.abs(off_wide) <= 1) & (jnp.abs(off_high) <= 1)
            code = (off_time + 1) * 9 + (off_high + 1) * 3 + (off_wide + 1)
            listed = jnp.right_shift(bits, jnp.where(near, code, 0)) & 1
            flag = jnp.where(near, listed, 0) * (has_f * has_s)
            bias_ref[start : start + length, place * rows : (place + 1) * rows] = jnp.where(
                flag == 1, jnp.float32(0), jnp.float32(NEG)
            )
            start += length


def lanes_of(head):
    return slice(head * HD, (head + 1) * HD)


def head_rows(ref, head):
    return ref[0, :, :, lanes_of(head)].reshape(-1, HD)


def load_keys(own_ref, a_ref, b_ref, which, head):
    lanes = lanes_of(head)
    return jnp.concatenate(
        [head_rows(own_ref, head), a_ref[which, :, lanes], b_ref[which, :, lanes]], axis=0
    )


def dot_nt(a, b):
    return lax.dot_general(a, b, (((1,), (1,)), ((), ())), preferred_element_type=jnp.float32)


def local_stats(query, grad, key, value, bias):
    scores = dot_nt(key, query) * SCALE2 + bias
    grad_probs = dot_nt(value, grad)
    top = jnp.max(scores, axis=0, keepdims=True)
    expo = jnp.exp2(scores - top)
    total = jnp.sum(expo, axis=0, keepdims=True)
    delta = jnp.sum(expo * grad_probs, axis=0, keepdims=True) / total
    return expo, grad_probs, top, top + jnp.log2(total), delta


def own_kernel(sizes, window_ref, place_ref, q0, g0, k0, v0, ha, hb, part, expo_out, gp_out, bias_ref):
    fill_bias(bias_ref, (0,), window_ref, place_ref, *sizes)
    for head in range(part.shape[0]):
        key = load_keys(k0, ha, hb, 0, head)
        value = load_keys(v0, ha, hb, 1, head)
        expo, grad_probs, top, lse, delta = local_stats(
            head_rows(q0, head), head_rows(g0, head), key, value, bias_ref[...]
        )
        part[head] = jnp.concatenate([lse, delta, top], axis=0)
        expo_out[head] = expo
        gp_out[head] = grad_probs


def near_kernel(sizes, window_ref, place_ref, qa, qb, ga, gb, k0, v0, ha, hb, own_part, part, a_out, b_out, c_out, d_out, expo_out, gp_out, bias_ref):
    rows = sizes[2] * sizes[3]
    fill_bias(bias_ref, (1, 2), window_ref, place_ref, *sizes)
    far_slot_a = ((place_ref[0] & 3) == 0) | ((place_ref[0] & 3) == 3)
    for head in range(part.shape[0]):
        key = load_keys(k0, ha, hb, 0, head)
        value = load_keys(v0, ha, hb, 1, head)
        query = jnp.concatenate([head_rows(qa, head), head_rows(qb, head)], axis=0)
        grad = jnp.concatenate([head_rows(ga, head), head_rows(gb, head)], axis=0)
        expo, grad_probs, top, lse, delta = local_stats(query, grad, key, value, bias_ref[...])
        expo_out[head] = expo
        gp_out[head] = grad_probs
        own = own_part[head][0:2]
        near = jnp.concatenate([lse, delta, top], axis=0)
        part[head] = near
        part_a = near[0:2, :rows]
        part_b = near[0:2, rows:]
        a_out[head] = jnp.concatenate([own, part_a], axis=0)
        b_out[head] = jnp.concatenate([own, part_b], axis=0)
        c_out[head] = jnp.where(far_slot_a, part_a, part_b)
        d_out[head] = jnp.where(far_slot_a, part_b, part_a)


def merge(parts):
    top = parts[0][0]
    for lse, _ in parts[1:]:
        top = jnp.maximum(top, lse)
    weight_sum = jnp.zeros_like(top)
    delta_sum = jnp.zeros_like(top)
    for lse, delta in parts:
        weight = jnp.exp2(lse - top)
        weight_sum = weight_sum + weight
        delta_sum = delta_sum + weight * delta
    return jnp.maximum(top + jnp.log2(weight_sum), FLOOR), delta_sum / weight_sum


def halo_kernel(sizes, place_ref, q0, qa, qb, g0, ga, gb, e0, p0, en, pn, own_st, near_st, a_st, b_st, c_st, d_st, ra_out, rb_out, row_out):
    frame_count, strip_count, height, strip = sizes
    rows = height * strip
    half = height * TW
    frame, step_f, _, has_fa, has_fb, _, _ = position_facts(place_ref, frame_count, strip_count)
    beyond_a = frame + 2 * step_f
    beyond_b = frame - 2 * step_f
    has_ba = (beyond_a >= 0) & (beyond_a < frame_count)
    has_bb = (beyond_b >= 0) & (beyond_b < frame_count)
    far_slot_a = ((frame & 3) == 0) | ((frame & 3) == 3)

    def part(block, row, exists):
        lse = block[row : row + 1, :]
        return (lse if exists is None else jnp.where(exists, lse, NEG), block[row + 1 : row + 2, :])

    for head in range(own_st.shape[0]):
        own, near, from_a, from_b, from_c, from_d = (
            r[head] for r in (own_st, near_st, a_st, b_st, c_st, d_st)
        )
        near_a = near[:, :rows]
        near_b = near[:, rows:]
        far_a = jnp.where(far_slot_a, from_c, from_d)
        far_b = jnp.where(far_slot_a, from_d, from_c)
        merged = [
            merge([part(own, 0, None), part(from_a, 2, has_fa == 1), part(from_b, 2, has_fb == 1)]),
            merge([part(near_a, 0, None), part(from_a, 0, has_fa == 1), part(far_a, 0, has_ba)]),
            merge([part(near_b, 0, None), part(from_b, 0, has_fb == 1), part(far_b, 0, has_bb)]),
        ]
        lse = jnp.concatenate([m[0] for m in merged], axis=1)
        delta = jnp.concatenate([m[1] for m in merged], axis=1)
        top = jnp.concatenate([own[2:3], near_a[2:3], near_b[2:3]], axis=1)
        factor = jnp.exp2(top - lse)
        row_out[head] = jnp.concatenate([factor, delta], axis=0)
        key_part, value_part = head_grads(
            head, slice(rows, rows + 2 * half), factor, delta, q0, qa, qb, g0, ga, gb, e0, p0, en, pn
        )
        lanes = lanes_of(head)
        for out, lo in ((ra_out, 0), (rb_out, half)):
            out[0, :, lanes] = key_part[lo : lo + half].astype(jnp.bfloat16)
            out[1, :, lanes] = value_part[lo : lo + half].astype(jnp.bfloat16)


def head_grads(head, keys, factor, delta, q0, qa, qb, g0, ga, gb, e0, p0, en, pn):
    query = jnp.concatenate([head_rows(r, head) for r in (q0, qa, qb)], axis=0)
    grad = jnp.concatenate([head_rows(r, head) for r in (g0, ga, gb)], axis=0)
    expo = jnp.concatenate([e0[head, keys, :], en[head, keys, :]], axis=1)
    grad_probs = jnp.concatenate([p0[head, keys, :], pn[head, keys, :]], axis=1)
    probs = expo * factor
    grad_scores = (probs * (grad_probs - delta)).astype(jnp.bfloat16)
    value_part = jnp.dot(probs.astype(jnp.bfloat16), grad, preferred_element_type=jnp.float32)
    key_part = jnp.dot(grad_scores, query, preferred_element_type=jnp.float32) * SCALE
    return key_part, value_part


def main_kernel(sizes, row_st, q0, qa, qb, g0, ga, gb, e0, p0, en, pn, dk_out, dv_out):
    rows = sizes[2] * sizes[3]
    for head in range(row_st.shape[0]):
        row = row_st[head]
        key_part, value_part = head_grads(
            head, slice(0, rows), row[0:1], row[1:2], q0, qa, qb, g0, ga, gb, e0, p0, en, pn
        )
        dk_out[:, lanes_of(head)] = key_part
        dv_out[:, lanes_of(head)] = value_part


def finish_kernel(sizes, lanes, place_ref, dk, dv, ra, rb, dk_out, dv_out):
    _, _, height, strip = sizes
    even = (place_ref[1] & 1) == 0
    span = pl.ds(pl.multiple_of(pl.program_id(0) * lanes, lanes), lanes)
    for which, (part, out) in enumerate(((dk, dk_out), (dv, dv_out))):
        from_a = ra[which, :, span].astype(jnp.float32).reshape(height, TW, lanes)
        from_b = rb[which, :, span].astype(jnp.float32).reshape(height, TW, lanes)
        full = part[:, span].reshape(height, strip, lanes)
        left = full[:, :TW] + jnp.where(even, from_b, from_a)
        right = full[:, TW:] + jnp.where(even, from_a, from_b)
        out[0] = jnp.concatenate([left, right], axis=1).astype(jnp.bfloat16)


def vmem(value):
    return pltpu.with_memory_space_constraint(value, pltpu.VMEM)


def on_device(queries, keys, values, grad_out, window):
    _, height, strip, chans = queries.shape
    heads = chans // HD
    rows = height * strip
    half = height * TW
    ext = rows + 2 * half
    frame_count = lax.axis_size("frame")
    strip_count = lax.axis_size("tile")
    sizes = (frame_count, strip_count, height, strip)
    frame_even, frame_odd, far_c, far_d = pair_lists(frame_count)
    tile_even, tile_odd, _, _ = pair_lists(strip_count)
    frame_pos = lax.axis_index("frame")
    strip_pos = lax.axis_index("tile")
    place = jnp.stack([frame_pos, strip_pos]).astype(jnp.int32)

    qa = swap(queries, "frame", frame_even)
    qb = swap(queries, "frame", frame_odd)
    ga = swap(grad_out, "frame", frame_even)
    gb = swap(grad_out, "frame", frame_odd)

    even = (strip_pos & 1) == 0
    start_a = jnp.where(even, strip - TW, 0)
    start_b = jnp.where(even, 0, strip - TW)

    def edge(start):
        cut = [lax.dynamic_slice_in_dim(x[0], start, TW, axis=1).reshape(half, chans) for x in (keys, values)]
        return jnp.stack(cut)

    ha = swap(edge(start_a), "tile", tile_even)
    hb = swap(edge(start_b), "tile", tile_odd)

    smem = pl.BlockSpec(memory_space=pltpu.SMEM)
    whole = pl.BlockSpec(memory_space=pltpu.VMEM)

    def call(kernel, name, scalars, arrays, outs, scratch=()):
        return pl.pallas_call(
            lambda *refs: kernel(sizes, *refs),
            name=name,
            in_specs=[smem] * len(scalars) + [whole] * len(arrays),
            out_specs=[whole] * len(outs),
            out_shape=[pltpu.VMEM(shape, dtype) for shape, dtype in outs],
            scratch_shapes=list(scratch),
            compiler_params=pltpu.CompilerParams(vmem_limit_bytes=KERNEL_VMEM),
        )(*scalars, *[vmem(x) for x in arrays])

    f32 = jnp.float32
    part, e0, p0 = call(
        own_kernel,
        "own_stats",
        (window, place),
        (queries, grad_out, keys, values, ha, hb),
        [((heads, 3, rows), f32), ((heads, ext, rows), f32), ((heads, ext, rows), f32)],
        [pltpu.VMEM((ext, rows), f32)],
    )
    near, a_st, b_st, c_st, d_st, en, pn = call(
        near_kernel,
        "near_stats",
        (window, place),
        (qa, qb, ga, gb, keys, values, ha, hb, part),
        [((heads, 3, 2 * rows), f32)]
        + [((heads, n, rows), f32) for n in (4, 4, 2, 2)]
        + [((heads, ext, 2 * rows), f32)] * 2,
        [pltpu.VMEM((ext, 2 * rows), f32)],
    )
    a_st = swap(a_st, "frame", frame_even)
    b_st = swap(b_st, "frame", frame_odd)
    if far_c:
        c_st = swap(c_st, "frame", far_c)
    if far_d:
        d_st = swap(d_st, "frame", far_d)

    data = (queries, qa, qb, grad_out, ga, gb, e0, p0, en, pn)
    ra, rb, row = call(
        halo_kernel,
        "halo_grads",
        (place,),
        data + (part, near, a_st, b_st, c_st, d_st),
        [((2, half, chans), jnp.bfloat16)] * 2 + [((heads, 2, 3 * rows), f32)],
    )
    ra = swap(ra, "tile", tile_even)
    rb = swap(rb, "tile", tile_odd)
    dk, dv = call(main_kernel, "main_grads", (), (row,) + data, [((rows, chans), f32)] * 2)

    lanes = chans // FINISH_STEPS
    out_spec = pl.BlockSpec((1, height, strip, lanes), lambda i: (0, 0, 0, i))
    return pl.pallas_call(
        lambda *refs: finish_kernel(sizes, lanes, *refs),
        name="finish",
        grid=(FINISH_STEPS,),
        compiler_params=pltpu.CompilerParams(vmem_limit_bytes=KERNEL_VMEM),
        in_specs=[smem] + [whole] * 4,
        out_specs=[out_spec, out_spec],
        out_shape=[jax.ShapeDtypeStruct(keys.shape, jnp.bfloat16)] * 2,
    )(place, vmem(dk), vmem(dv), vmem(ra), vmem(rb))


def solution(mesh):
    spec = P(("clip", "frame"), None, "tile", None)
    return jax.shard_map(
        on_device,
        mesh=mesh,
        in_specs=(spec, spec, spec, spec, P()),
        out_specs=(spec, spec),
        check_vma=False,
    )
```

```python
import math

import jax
import jax.numpy as jnp
from jax import lax
from jax.experimental import pallas as pl
from jax.experimental.pallas import tpu as pltpu
from jax.sharding import PartitionSpec as P

HD = 128
TH = 4
TW = 8
FINISH_STEPS = 4
FLOPS = 1_500_000_000
KERNEL_VMEM = 16 << 20
NEG = -1e30
FLOOR = -1e29
SCALE = HD ** (-0.5)
SCALE2 = SCALE * math.log2(math.e)


def pair_lists(count):
    even = [(i, i + 1) for i in range(0, count - 1, 2)]
    odd = [(i, i + 1) for i in range(1, count - 1, 2)]
    far_a = [(i, i + 2) for i in range(count - 2) if i % 4 in (0, 1)]
    far_b = [(i, i + 2) for i in range(count - 2) if i % 4 in (2, 3)]
    return [pairs + [(j, i) for i, j in pairs] for pairs in (even, odd, far_a, far_b)]


def swap(value, axis, pairs):
    return lax.ppermute(value, axis, pairs)


def bit_table(window_ref):
    bits = jnp.int32(0)
    for i in range(window_ref.shape[0]):
        code = (window_ref[i, 0] + 1) * 9 + (window_ref[i, 1] + 1) * 3 + (window_ref[i, 2] + 1)
        bits = bits | jnp.left_shift(jnp.int32(1), code)
    return bits


def position_facts(place_ref, frame_count, strip_count):
    frame = place_ref[0]
    strip = place_ref[1]
    step_f = 1 - 2 * (frame & 1)
    step_s = 1 - 2 * (strip & 1)
    return (
        frame,
        step_f,
        step_s,
        ((frame + step_f >= 0) & (frame + step_f < frame_count)).astype(jnp.int32),
        ((frame - step_f >= 0) & (frame - step_f < frame_count)).astype(jnp.int32),
        ((strip + step_s >= 0) & (strip + step_s < strip_count)).astype(jnp.int32),
        ((strip - step_s >= 0) & (strip - step_s < strip_count)).astype(jnp.int32),
    )


def fill_bias(bias_ref, slots, window_ref, place_ref, frame_count, strip_count, height, strip):
    bits = bit_table(window_ref)
    _, step_f, step_s, has_fa, has_fb, has_sa, has_sb = position_facts(
        place_ref, frame_count, strip_count
    )
    rows = height * strip
    half = height * TW
    tiles = strip // TW
    col_a = jnp.where(step_s > 0, tiles, -1)
    col_b = jnp.where(step_s > 0, -1, tiles)
    frames = ((0, 1), (-step_f, has_fa), (step_f, has_fb))
    for place, slot in enumerate(slots):
        off_time, has_f = frames[slot]
        start = 0
        for length, wide, k_col, has_s in (
            (rows, strip, None, 1),
            (half, TW, col_a, has_sa),
            (half, TW, col_b, has_sb),
        ):
            key_idx = lax.broadcasted_iota(jnp.int32, (length, rows), 0)
            query_idx = lax.broadcasted_iota(jnp.int32, (length, rows), 1)
            off_high = key_idx // (wide * TH) - query_idx // (strip * TH)
            k_wide = (key_idx % wide) // TW if k_col is None else k_col
            off_wide = k_wide - (query_idx % strip) // TW
            near = (jnp.abs(off_wide) <= 1) & (jnp.abs(off_high) <= 1)
            code = (off_time + 1) * 9 + (off_high + 1) * 3 + (off_wide + 1)
            listed = jnp.right_shift(bits, jnp.where(near, code, 0)) & 1
            flag = jnp.where(near, listed, 0) * (has_f * has_s)
            bias_ref[start : start + length, place * rows : (place + 1) * rows] = jnp.where(
                flag == 1, jnp.float32(0), jnp.float32(NEG)
            )
            start += length


def lanes_of(head):
    return slice(head * HD, (head + 1) * HD)


def head_rows(ref, head):
    return ref[0, :, :, lanes_of(head)].reshape(-1, HD)


def load_keys(own_ref, a_ref, b_ref, which, head):
    lanes = lanes_of(head)
    return jnp.concatenate(
        [head_rows(own_ref, head), a_ref[which, :, lanes], b_ref[which, :, lanes]], axis=0
    )


def dot_nt(a, b):
    return lax.dot_general(a, b, (((1,), (1,)), ((), ())), preferred_element_type=jnp.float32)


def edges_kernel(sizes, place_ref, k0, v0, a_out, b_out):
    _, _, height, strip = sizes
    even = (place_ref[1] & 1) == 0
    for which, ref in enumerate((k0, v0)):
        left = ref[0, :, :TW, :].reshape(height * TW, -1)
        right = ref[0, :, strip - TW :, :].reshape(height * TW, -1)
        a_out[which] = jnp.where(even, right, left)
        b_out[which] = jnp.where(even, left, right)


def scores_kernel(sizes, window_ref, place_ref, q0, qa, qb, g0, k0, v0, ha, hb, expo_out, gp_out, st_out, delta_out, bias_ref):
    rows = sizes[2] * sizes[3]
    fill_bias(bias_ref, (0, 1, 2), window_ref, place_ref, *sizes)
    for head in range(st_out.shape[0]):
        key = load_keys(k0, ha, hb, 0, head)
        value = load_keys(v0, ha, hb, 1, head)
        query = jnp.concatenate([head_rows(r, head) for r in (q0, qa, qb)], axis=0)
        scores = dot_nt(key, query) * SCALE2 + bias_ref[...]
        grad_probs = dot_nt(value, head_rows(g0, head))
        top = jnp.max(scores, axis=0, keepdims=True)
        expo = jnp.exp2(scores - top)
        total = jnp.sum(expo, axis=0, keepdims=True)
        inverse = 1.0 / total
        expo_out[head] = expo
        gp_out[head] = grad_probs
        st_out[head] = jnp.concatenate([top + jnp.log2(total), top, inverse], axis=0)
        delta_out[head] = jnp.sum(expo[:, :rows] * grad_probs, axis=0, keepdims=True) * inverse[:, :rows]


def deltas_kernel(sizes, place_ref, ga, gb, v0, ha, hb, expo, st, own_delta, gp_out, delta_out, a_out, b_out, c_out, d_out):
    rows = sizes[2] * sizes[3]
    far_slot_a = ((place_ref[0] & 3) == 0) | ((place_ref[0] & 3) == 3)
    for head in range(st.shape[0]):
        value = load_keys(v0, ha, hb, 1, head)
        grad = jnp.concatenate([head_rows(ga, head), head_rows(gb, head)], axis=0)
        grad_probs = dot_nt(value, grad)
        gp_out[head] = grad_probs
        stat = st[head]
        near = jnp.sum(expo[head, :, rows:] * grad_probs, axis=0, keepdims=True) * stat[2:3, rows:]
        delta = jnp.concatenate([own_delta[head], near], axis=1)
        delta_out[head] = delta
        own, part_a, part_b = (
            jnp.concatenate([x[:, i * rows : (i + 1) * rows] for x in (stat[0:1], delta)], axis=0)
            for i in range(3)
        )
        a_out[head] = jnp.concatenate([own, part_a], axis=0)
        b_out[head] = jnp.concatenate([own, part_b], axis=0)
        c_out[head] = jnp.where(far_slot_a, part_a, part_b)
        d_out[head] = jnp.where(far_slot_a, part_b, part_a)


def merge(parts):
    top = parts[0][0]
    for lse, _ in parts[1:]:
        top = jnp.maximum(top, lse)
    weight_sum = jnp.zeros_like(top)
    delta_sum = jnp.zeros_like(top)
    for lse, delta in parts:
        weight = jnp.exp2(lse - top)
        weight_sum = weight_sum + weight
        delta_sum = delta_sum + weight * delta
    return jnp.maximum(top + jnp.log2(weight_sum), FLOOR), delta_sum / weight_sum


def halo_kernel(sizes, place_ref, q0, qa, qb, g0, ga, gb, expo, p0, pn, st, local_delta, a_st, b_st, c_st, d_st, rb_out, ra_out, row_out):
    frame_count, strip_count, height, strip = sizes
    rows = height * strip
    half = height * TW
    frame, step_f, _, has_fa, has_fb, _, _ = position_facts(place_ref, frame_count, strip_count)
    beyond_a = frame + 2 * step_f
    beyond_b = frame - 2 * step_f
    has_ba = (beyond_a >= 0) & (beyond_a < frame_count)
    has_bb = (beyond_b >= 0) & (beyond_b < frame_count)
    far_slot_a = ((frame & 3) == 0) | ((frame & 3) == 3)

    def part(block, row, exists):
        return (jnp.where(exists, block[row : row + 1, :], NEG), block[row + 1 : row + 2, :])

    for head in range(st.shape[0]):
        stat, local, from_a, from_b, from_c, from_d = (
            r[head] for r in (st, local_delta, a_st, b_st, c_st, d_st)
        )
        own, near_a, near_b = (
            (stat[0:1, i * rows : (i + 1) * rows], local[:, i * rows : (i + 1) * rows]) for i in range(3)
        )
        far_a = jnp.where(far_slot_a, from_c, from_d)
        far_b = jnp.where(far_slot_a, from_d, from_c)
        merged = [
            merge([own, part(from_a, 2, has_fa == 1), part(from_b, 2, has_fb == 1)]),
            merge([near_a, part(from_a, 0, has_fa == 1), part(far_a, 0, has_ba)]),
            merge([near_b, part(from_b, 0, has_fb == 1), part(far_b, 0, has_bb)]),
        ]
        lse = jnp.concatenate([m[0] for m in merged], axis=1)
        delta = jnp.concatenate([m[1] for m in merged], axis=1)
        row = jnp.concatenate([jnp.exp2(stat[1:2] - lse), delta], axis=0)
        row_out[head] = row
        key_part, value_part = head_grads(
            head, slice(rows, rows + 2 * half), row, q0, qa, qb, g0, ga, gb, expo, p0, pn
        )
        lanes = lanes_of(head)
        for out, lo in ((ra_out, 0), (rb_out, half)):
            out[0, :, lanes] = key_part[lo : lo + half].astype(jnp.bfloat16)
            out[1, :, lanes] = value_part[lo : lo + half].astype(jnp.bfloat16)


def head_grads(head, keys, row, q0, qa, qb, g0, ga, gb, expo_ref, p0, pn):
    query = jnp.concatenate([head_rows(r, head) for r in (q0, qa, qb)], axis=0)
    grad = jnp.concatenate([head_rows(r, head) for r in (g0, ga, gb)], axis=0)
    expo = expo_ref[head, keys, :]
    grad_probs = jnp.concatenate([p0[head, keys, :], pn[head, keys, :]], axis=1)
    factor = row[0:1]
    probs = expo * factor
    grad_scores = (expo * (factor * SCALE) * (grad_probs - row[1:2])).astype(jnp.bfloat16)
    value_part = jnp.dot(probs.astype(jnp.bfloat16), grad, preferred_element_type=jnp.float32)
    key_part = jnp.dot(grad_scores, query, preferred_element_type=jnp.float32)
    return key_part, value_part


def main_kernel(sizes, row_st, q0, qa, qb, g0, ga, gb, expo, p0, pn, dk_out, dv_out):
    rows = sizes[2] * sizes[3]
    for head in range(row_st.shape[0]):
        key_part, value_part = head_grads(
            head, slice(0, rows), row_st[head], q0, qa, qb, g0, ga, gb, expo, p0, pn
        )
        lanes = lanes_of(head)
        dk_out[:, lanes] = key_part
        dv_out[:, lanes] = value_part


def finish_kernel(sizes, step_rows, place_ref, rb, ra, dk, dv, dk_out, dv_out):
    _, _, height, strip = sizes
    even = (place_ref[1] & 1) == 0
    step = pl.program_id(0)
    edge = pl.ds(pl.multiple_of(step * step_rows * TW, step_rows * TW), step_rows * TW)
    span = pl.ds(pl.multiple_of(step * step_rows * strip, step_rows * strip), step_rows * strip)
    for which, (part, out) in enumerate(((dk, dk_out), (dv, dv_out))):
        from_a = ra[which, edge, :].astype(jnp.float32).reshape(step_rows, TW, -1)
        from_b = rb[which, edge, :].astype(jnp.float32).reshape(step_rows, TW, -1)
        full = part[span, :].reshape(step_rows, strip, -1)
        left = full[:, :TW] + jnp.where(even, from_b, from_a)
        right = full[:, TW:] + jnp.where(even, from_a, from_b)
        out[0] = jnp.concatenate([left, right], axis=1).astype(jnp.bfloat16)


def vmem(value):
    return pltpu.with_memory_space_constraint(value, pltpu.VMEM)


def on_device(queries, keys, values, grad_out, window):
    _, height, strip, chans = queries.shape
    heads = chans // HD
    rows = height * strip
    half = height * TW
    ext = rows + 2 * half
    frame_count = lax.axis_size("frame")
    strip_count = lax.axis_size("tile")
    sizes = (frame_count, strip_count, height, strip)
    frame_even, frame_odd, far_c, far_d = pair_lists(frame_count)
    tile_even, tile_odd, _, _ = pair_lists(strip_count)
    frame_pos = lax.axis_index("frame")
    strip_pos = lax.axis_index("tile")
    place = jnp.stack([frame_pos, strip_pos]).astype(jnp.int32)

    qa = swap(queries, "frame", frame_even)
    qb = swap(queries, "frame", frame_odd)
    ga = swap(grad_out, "frame", frame_even)
    gb = swap(grad_out, "frame", frame_odd)

    smem = pl.BlockSpec(memory_space=pltpu.SMEM)
    whole = pl.BlockSpec(memory_space=pltpu.VMEM)

    def call(kernel, name, scalars, arrays, outs, scratch=(), flops=FLOPS):
        return pl.pallas_call(
            lambda *refs: kernel(sizes, *refs),
            name=name,
            in_specs=[smem] * len(scalars) + [whole] * len(arrays),
            out_specs=[whole] * len(outs),
            out_shape=[pltpu.VMEM(shape, dtype) for shape, dtype in outs],
            scratch_shapes=list(scratch),
            cost_estimate=pl.CostEstimate(flops=flops, transcendentals=0, bytes_accessed=0),
            compiler_params=pltpu.CompilerParams(vmem_limit_bytes=KERNEL_VMEM),
        )(*scalars, *[vmem(x) for x in arrays])

    f32 = jnp.float32
    ea, eb = call(
        edges_kernel, "edges", (place,), (keys, values), [((2, half, chans), jnp.bfloat16)] * 2
    )
    ha = swap(ea, "tile", tile_even)
    hb = swap(eb, "tile", tile_odd)
    expo, p0, st, own_delta = call(
        scores_kernel,
        "scores",
        (window, place),
        (queries, qa, qb, grad_out, keys, values, ha, hb),
        [
            ((heads, ext, 3 * rows), f32),
            ((heads, ext, rows), f32),
            ((heads, 3, 3 * rows), f32),
            ((heads, 1, rows), f32),
        ],
        [pltpu.VMEM((ext, 3 * rows), f32)],
    )
    pn, local_delta, a_st, b_st, c_st, d_st = call(
        deltas_kernel,
        "deltas",
        (place,),
        (ga, gb, values, ha, hb, expo, st, own_delta),
        [((heads, ext, 2 * rows), f32), ((heads, 1, 3 * rows), f32)]
        + [((heads, n, rows), f32) for n in (4, 4, 2, 2)],
    )
    a_st = swap(a_st, "frame", frame_even)
    b_st = swap(b_st, "frame", frame_odd)
    if far_c:
        c_st = swap(c_st, "frame", far_c)
    if far_d:
        d_st = swap(d_st, "frame", far_d)

    data = (queries, qa, qb, grad_out, ga, gb, expo, p0, pn)
    rb, ra, row = call(
        halo_kernel,
        "halo_grads",
        (place,),
        data + (st, local_delta, a_st, b_st, c_st, d_st),
        [((2, half, chans), jnp.bfloat16)] * 2 + [((heads, 2, 3 * rows), f32)],
    )
    rb = swap(rb, "tile", tile_odd)
    ra = swap(ra, "tile", tile_even)
    dk, dv = call(
        main_kernel,
        "main_grads",
        (),
        (row,) + data,
        [((rows, chans), f32)] * 2,
    )

    step_rows = height // FINISH_STEPS
    out_spec = pl.BlockSpec((1, step_rows, strip, chans), lambda i: (0, i, 0, 0))
    return pl.pallas_call(
        lambda *refs: finish_kernel(sizes, step_rows, *refs),
        name="finish",
        grid=(FINISH_STEPS,),
        compiler_params=pltpu.CompilerParams(vmem_limit_bytes=KERNEL_VMEM),
        in_specs=[smem] + [whole] * 4,
        out_specs=[out_spec, out_spec],
        out_shape=[jax.ShapeDtypeStruct(keys.shape, jnp.bfloat16)] * 2,
    )(place, vmem(rb), vmem(ra), vmem(dk), vmem(dv))


def solution(mesh):
    spec = P(("clip", "frame"), None, "tile", None)
    return jax.shard_map(
        on_device,
        mesh=mesh,
        in_specs=(spec, spec, spec, spec, P()),
        out_specs=(spec, spec),
        check_vma=False,
    )
```

```python
import math

import jax
import jax.numpy as jnp
from jax import lax
from jax.experimental import pallas as pl
from jax.experimental.pallas import tpu as pltpu
from jax.sharding import PartitionSpec as P

HD = 128
TH = 4
TW = 8
FINISH_STEPS = 4
FLOPS = 1_000_000_000
KERNEL_VMEM = 16 << 20
NEG = -1e30
FLOOR = -1e29
SCALE = HD ** (-0.5)
SCALE2 = SCALE * math.log2(math.e)


def pair_lists(count):
    even = [(i, i + 1) for i in range(0, count - 1, 2)]
    odd = [(i, i + 1) for i in range(1, count - 1, 2)]
    far_a = [(i, i + 2) for i in range(count - 2) if i % 4 in (0, 1)]
    far_b = [(i, i + 2) for i in range(count - 2) if i % 4 in (2, 3)]
    return [pairs + [(j, i) for i, j in pairs] for pairs in (even, odd, far_a, far_b)]


def swap(value, axis, pairs):
    return lax.ppermute(value, axis, pairs)


def bit_table(window_ref):
    bits = jnp.int32(0)
    for i in range(window_ref.shape[1]):
        code = (window_ref[0, i] + 1) * 9 + (window_ref[1, i] + 1) * 3 + (window_ref[2, i] + 1)
        bits = bits | jnp.left_shift(jnp.int32(1), code)
    return bits


def position_facts(place_ref, frame_count, strip_count):
    frame = place_ref[0]
    strip = place_ref[1]
    step_f = 1 - 2 * (frame & 1)
    step_s = 1 - 2 * (strip & 1)
    return (
        frame,
        step_f,
        step_s,
        ((frame + step_f >= 0) & (frame + step_f < frame_count)).astype(jnp.int32),
        ((frame - step_f >= 0) & (frame - step_f < frame_count)).astype(jnp.int32),
        ((strip + step_s >= 0) & (strip + step_s < strip_count)).astype(jnp.int32),
        ((strip - step_s >= 0) & (strip - step_s < strip_count)).astype(jnp.int32),
    )


def fill_bias(bias_ref, slots, window_ref, place_ref, frame_count, strip_count, height, strip):
    bits = bit_table(window_ref)
    _, step_f, step_s, has_fa, has_fb, has_sa, has_sb = position_facts(
        place_ref, frame_count, strip_count
    )
    rows = height * strip
    half = height * TW
    tiles = strip // TW
    col_a = jnp.where(step_s > 0, tiles, -1)
    col_b = jnp.where(step_s > 0, -1, tiles)
    frames = ((0, 1), (-step_f, has_fa), (step_f, has_fb))
    for place, slot in enumerate(slots):
        off_time, has_f = frames[slot]
        start = 0
        for length, wide, k_col, has_s in (
            (rows, strip, None, 1),
            (half, TW, col_a, has_sa),
            (half, TW, col_b, has_sb),
        ):
            key_idx = lax.broadcasted_iota(jnp.int32, (length, rows), 0)
            query_idx = lax.broadcasted_iota(jnp.int32, (length, rows), 1)
            off_high = key_idx // (wide * TH) - query_idx // (strip * TH)
            k_wide = (key_idx % wide) // TW if k_col is None else k_col
            off_wide = k_wide - (query_idx % strip) // TW
            near = (jnp.abs(off_wide) <= 1) & (jnp.abs(off_high) <= 1)
            code = (off_time + 1) * 9 + (off_high + 1) * 3 + (off_wide + 1)
            listed = jnp.right_shift(bits, jnp.where(near, code, 0)) & 1
            flag = jnp.where(near, listed, 0) * (has_f * has_s)
            bias_ref[start : start + length, place * rows : (place + 1) * rows] = jnp.where(
                flag == 1, jnp.float32(0), jnp.float32(NEG)
            )
            start += length


def lanes_of(head):
    return slice(head * HD, (head + 1) * HD)


def head_rows(ref, which, head):
    return ref[which, :, :, lanes_of(head)].reshape(-1, HD)


def load_keys(kv, a_ref, b_ref, which, head):
    lanes = lanes_of(head)
    return jnp.concatenate(
        [head_rows(kv, which, head), a_ref[which, :, lanes], b_ref[which, :, lanes]], axis=0
    )


def dot_nt(a, b):
    return lax.dot_general(a, b, (((1,), (1,)), ((), ())), preferred_element_type=jnp.float32)


def run_copies(pairs, sems):
    copies = [pltpu.make_async_copy(src, dst, sems.at[i]) for i, (src, dst) in enumerate(pairs)]
    for copy in copies:
        copy.start()
    for copy in copies:
        copy.wait()


def pair_kernel(q_in, g_in, out, sems):
    run_copies([(q_in.at[0], out.at[0]), (g_in.at[0], out.at[1])], sems)


def stage_kernel(sizes, place_ref, k_in, v_in, out, a_out, b_out, sems):
    _, _, height, strip = sizes
    even = (place_ref[1] & 1) == 0
    start_a = pl.multiple_of(jnp.where(even, strip - TW, 0), TW)
    start_b = pl.multiple_of(jnp.where(even, 0, strip - TW), TW)
    pairs = []
    for edge, start in ((a_out, start_a), (b_out, start_b)):
        for which, ref in enumerate((k_in, v_in)):
            for row in range(height):
                pairs.append((ref.at[0, row, pl.ds(start, TW), :], edge.at[which, row * TW : (row + 1) * TW, :]))
    run_copies(pairs + [(k_in.at[0], out.at[0]), (v_in.at[0], out.at[1])], sems)


def local_stats(head, frames, kv, ha, hb, bias):
    query, grad = (
        jnp.concatenate([head_rows(ref, which, head) for ref in frames], axis=0) for which in (0, 1)
    )
    scores = dot_nt(load_keys(kv, ha, hb, 0, head), query) * SCALE2 + bias
    grad_probs = dot_nt(load_keys(kv, ha, hb, 1, head), grad)
    top = jnp.max(scores, axis=0, keepdims=True)
    expo = jnp.exp2(scores - top)
    total = jnp.sum(expo, axis=0, keepdims=True)
    delta = jnp.sum(expo * grad_probs, axis=0, keepdims=True) / total
    return expo, grad_probs, jnp.concatenate([top + jnp.log2(total), delta, top], axis=0)


def own_kernel(sizes, window_ref, place_ref, own, kv, ha, hb, st_out, expo_out, gp_out, bias_ref):
    fill_bias(bias_ref, (0,), window_ref, place_ref, *sizes)
    for head in range(st_out.shape[0]):
        expo_out[head], gp_out[head], st_out[head] = local_stats(head, (own,), kv, ha, hb, bias_ref[...])


def near_kernel(sizes, window_ref, place_ref, near_a, near_b, kv, ha, hb, own_st, st_out, a_out, b_out, c_out, d_out, expo_out, gp_out, bias_ref):
    rows = sizes[2] * sizes[3]
    fill_bias(bias_ref, (1, 2), window_ref, place_ref, *sizes)
    far_slot_a = ((place_ref[0] & 3) == 0) | ((place_ref[0] & 3) == 3)
    for head in range(st_out.shape[0]):
        expo_out[head], gp_out[head], near = local_stats(
            head, (near_a, near_b), kv, ha, hb, bias_ref[...]
        )
        st_out[head] = near
        own = own_st[head][0:2]
        part_a = near[0:2, :rows]
        part_b = near[0:2, rows:]
        a_out[head] = jnp.concatenate([own, part_a], axis=0)
        b_out[head] = jnp.concatenate([own, part_b], axis=0)
        c_out[head] = jnp.where(far_slot_a, part_a, part_b)
        d_out[head] = jnp.where(far_slot_a, part_b, part_a)


def merge(parts):
    top = parts[0][0]
    for lse, _ in parts[1:]:
        top = jnp.maximum(top, lse)
    weight_sum = jnp.zeros_like(top)
    delta_sum = jnp.zeros_like(top)
    for lse, delta in parts:
        weight = jnp.exp2(lse - top)
        weight_sum = weight_sum + weight
        delta_sum = delta_sum + weight * delta
    return jnp.maximum(top + jnp.log2(weight_sum), FLOOR), delta_sum / weight_sum


def halo_kernel(sizes, place_ref, c_st, d_st, b_st, a_st, own, near_a, near_b, e0, en, p0, pn, own_st, near_st, rb_out, ra_out, row_out):
    frame_count, strip_count, height, strip = sizes
    rows = height * strip
    half = height * TW
    frame, step_f, _, has_fa, has_fb, _, _ = position_facts(place_ref, frame_count, strip_count)
    beyond_a = frame + 2 * step_f
    beyond_b = frame - 2 * step_f
    has_ba = (beyond_a >= 0) & (beyond_a < frame_count)
    has_bb = (beyond_b >= 0) & (beyond_b < frame_count)
    far_slot_a = ((frame & 3) == 0) | ((frame & 3) == 3)

    def part(block, row, exists):
        return (jnp.where(exists, block[row : row + 1, :], NEG), block[row + 1 : row + 2, :])

    for head in range(own_st.shape[0]):
        from_a, from_b, from_c, from_d = (r[head] for r in (a_st, b_st, c_st, d_st))
        stat = jnp.concatenate([own_st[head], near_st[head]], axis=1)
        own_part, part_a, part_b = (
            (stat[0:1, i * rows : (i + 1) * rows], stat[1:2, i * rows : (i + 1) * rows]) for i in range(3)
        )
        far_a = jnp.where(far_slot_a, from_c, from_d)
        far_b = jnp.where(far_slot_a, from_d, from_c)
        merged = [
            merge([own_part, part(from_a, 2, has_fa == 1), part(from_b, 2, has_fb == 1)]),
            merge([part_a, part(from_a, 0, has_fa == 1), part(far_a, 0, has_ba)]),
            merge([part_b, part(from_b, 0, has_fb == 1), part(far_b, 0, has_bb)]),
        ]
        lse = jnp.concatenate([m[0] for m in merged], axis=1)
        delta = jnp.concatenate([m[1] for m in merged], axis=1)
        row = jnp.concatenate([jnp.exp2(stat[2:3] - lse), delta], axis=0)
        row_out[head] = row
        key_part, value_part = head_grads(
            head, slice(rows, rows + 2 * half), row, own, near_a, near_b, e0, en, p0, pn
        )
        lanes = lanes_of(head)
        for out, lo in ((ra_out, 0), (rb_out, half)):
            out[0, :, lanes] = key_part[lo : lo + half].astype(jnp.bfloat16)
            out[1, :, lanes] = value_part[lo : lo + half].astype(jnp.bfloat16)


def head_grads(head, keys, row, own, near_a, near_b, e0, en, p0, pn):
    query, grad = (
        jnp.concatenate([head_rows(r, which, head) for r in (own, near_a, near_b)], axis=0)
        for which in (0, 1)
    )
    expo = jnp.concatenate([e0[head, keys, :], en[head, keys, :]], axis=1)
    grad_probs = jnp.concatenate([p0[head, keys, :], pn[head, keys, :]], axis=1)
    factor = row[0:1]
    probs = expo * factor
    grad_scores = (expo * (factor * SCALE) * (grad_probs - row[1:2])).astype(jnp.bfloat16)
    value_part = jnp.dot(probs.astype(jnp.bfloat16), grad, preferred_element_type=jnp.float32)
    key_part = jnp.dot(grad_scores, query, preferred_element_type=jnp.float32)
    return key_part, value_part


def main_kernel(sizes, row_st, own, near_a, near_b, e0, en, p0, pn, dk_out, dv_out):
    rows = sizes[2] * sizes[3]
    for head in range(row_st.shape[0]):
        key_part, value_part = head_grads(
            head, slice(0, rows), row_st[head], own, near_a, near_b, e0, en, p0, pn
        )
        lanes = lanes_of(head)
        dk_out[:, lanes] = key_part
        dv_out[:, lanes] = value_part


def finish_kernel(sizes, place_ref, rb, ra, dk, dv, dk_out, dv_out, full_ref, sems):
    _, _, height, strip = sizes
    even = (place_ref[1] & 1) == 0
    count = height // FINISH_STEPS
    copies = []
    for step in range(FINISH_STEPS):
        lines = slice(step * count, (step + 1) * count)
        edge = slice(step * count * TW, (step + 1) * count * TW)
        span = slice(step * count * strip, (step + 1) * count * strip)
        for which, (part, out) in enumerate(((dk, dk_out), (dv, dv_out))):
            from_a = ra[which, edge, :].astype(jnp.float32).reshape(count, TW, -1)
            from_b = rb[which, edge, :].astype(jnp.float32).reshape(count, TW, -1)
            full = part[span, :].reshape(count, strip, -1)
            left = full[:, :TW] + jnp.where(even, from_b, from_a)
            right = full[:, TW:] + jnp.where(even, from_a, from_b)
            full_ref[which, lines] = jnp.concatenate([left, right], axis=1).astype(jnp.bfloat16)
            copy = pltpu.make_async_copy(
                full_ref.at[which, lines], out.at[0, lines], sems.at[2 * step + which]
            )
            copy.start()
            copies.append(copy)
    for copy in copies:
        copy.wait()


def vmem(value):
    return pltpu.with_memory_space_constraint(value, pltpu.VMEM)


def on_device(queries, keys, values, grad_out, window):
    _, height, strip, chans = queries.shape
    heads = chans // HD
    rows = height * strip
    half = height * TW
    ext = rows + 2 * half
    frame_count = lax.axis_size("frame")
    strip_count = lax.axis_size("tile")
    sizes = (frame_count, strip_count, height, strip)
    frame_even, frame_odd, far_c, far_d = pair_lists(frame_count)
    tile_even, tile_odd, _, _ = pair_lists(strip_count)
    frame_pos = lax.axis_index("frame")
    strip_pos = lax.axis_index("tile")
    place = jnp.stack([frame_pos, strip_pos]).astype(jnp.int32)

    smem = pl.BlockSpec(memory_space=pltpu.SMEM)
    whole = pl.BlockSpec(memory_space=pltpu.VMEM)
    raw = pl.BlockSpec(memory_space=pl.ANY)
    window = window.T

    def call(kernel, name, scalars, arrays, outs, scratch=(), flops=0):
        return pl.pallas_call(
            lambda *refs: kernel(sizes, *refs),
            name=name,
            in_specs=[smem] * len(scalars) + [whole] * len(arrays),
            out_specs=[whole] * len(outs),
            out_shape=[pltpu.VMEM(shape, dtype) for shape, dtype in outs],
            scratch_shapes=list(scratch),
            cost_estimate=pl.CostEstimate(flops=flops, transcendentals=0, bytes_accessed=0),
            compiler_params=pltpu.CompilerParams(vmem_limit_bytes=KERNEL_VMEM),
        )(*scalars, *[vmem(x) for x in arrays])

    def raw_call(kernel, name, arrays, scalars, outs, copies):
        return pl.pallas_call(
            kernel,
            name=name,
            in_specs=[smem] * len(scalars) + [raw] * len(arrays),
            out_specs=[whole] * len(outs),
            out_shape=[pltpu.VMEM(shape, jnp.bfloat16) for shape in outs],
            scratch_shapes=[pltpu.SemaphoreType.DMA((copies,))],
            compiler_params=pltpu.CompilerParams(vmem_limit_bytes=KERNEL_VMEM),
            cost_estimate=pl.CostEstimate(flops=0, transcendentals=0, bytes_accessed=0),
        )(*scalars, *[pltpu.with_memory_space_constraint(x, pltpu.HBM) for x in arrays])

    f32 = jnp.float32
    wide = queries.shape
    two = (2, height, strip, chans)
    edge = (2, half, chans)
    (own,) = raw_call(pair_kernel, "pair", (queries, grad_out), (), [two], 2)
    near_a = swap(own, "frame", frame_even)
    near_b = swap(own, "frame", frame_odd)
    kv, ea, eb = raw_call(
        lambda *refs: stage_kernel(sizes, *refs),
        "stage",
        (keys, values),
        (place,),
        [two, edge, edge],
        4 * height + 2,
    )
    hb = swap(eb, "tile", tile_odd)
    ha = swap(ea, "tile", tile_even)
    own_st, e0, p0 = call(
        own_kernel,
        "own_stats",
        (window, place),
        (own, kv, ha, hb),
        [((heads, 3, rows), f32), ((heads, ext, rows), f32), ((heads, ext, rows), f32)],
        [pltpu.VMEM((ext, rows), f32)],
    )
    near_st, a_st, b_st, c_st, d_st, en, pn = call(
        near_kernel,
        "near_stats",
        (window, place),
        (near_a, near_b, kv, ha, hb, own_st),
        [((heads, 3, 2 * rows), f32)]
        + [((heads, n, rows), f32) for n in (4, 4, 2, 2)]
        + [((heads, ext, 2 * rows), f32)] * 2,
        [pltpu.VMEM((ext, 2 * rows), f32)],
    )
    a_st = swap(a_st, "frame", frame_even)
    b_st = swap(b_st, "frame", frame_odd)
    if far_c:
        c_st = swap(c_st, "frame", far_c)
    if far_d:
        d_st = swap(d_st, "frame", far_d)

    data = (own, near_a, near_b, e0, en, p0, pn)
    rb, ra, row = call(
        halo_kernel,
        "halo_grads",
        (place,),
        (c_st, d_st, b_st, a_st) + data + (own_st, near_st),
        [(edge, jnp.bfloat16)] * 2 + [((heads, 2, 3 * rows), f32)],
    )
    rb = swap(rb, "tile", tile_odd)
    ra = swap(ra, "tile", tile_even)
    dk, dv = call(main_kernel, "main_grads", (), (row,) + data, [((rows, chans), f32)] * 2, flops=FLOPS)

    return pl.pallas_call(
        lambda *refs: finish_kernel(sizes, *refs),
        name="finish",
        compiler_params=pltpu.CompilerParams(vmem_limit_bytes=KERNEL_VMEM),
        in_specs=[smem] + [whole] * 4,
        out_specs=[raw, raw],
        out_shape=[jax.ShapeDtypeStruct(wide, jnp.bfloat16)] * 2,
        scratch_shapes=[
            pltpu.VMEM((2, height, strip, chans), jnp.bfloat16),
            pltpu.SemaphoreType.DMA((2 * FINISH_STEPS,)),
        ],
    )(place, vmem(rb), vmem(ra), vmem(dk), vmem(dv))


def solution(mesh):
    spec = P(("clip", "frame"), None, "tile", None)
    return jax.shard_map(
        on_device,
        mesh=mesh,
        in_specs=(spec, spec, spec, spec, P()),
        out_specs=(spec, spec),
        check_vma=False,
    )
```

```python
import math

import jax
import jax.numpy as jnp
from jax import lax
from jax.experimental import pallas as pl
from jax.experimental.pallas import tpu as pltpu
from jax.sharding import PartitionSpec as P

HD = 128
TH = 4
TW = 8
FINISH_STEPS = 4
FLOPS = 1_500_000_000
KERNEL_VMEM = 16 << 20
NEG = -1e30
FLOOR = -1e29
SCALE = HD ** (-0.5)
SCALE2 = SCALE * math.log2(math.e)


def pair_lists(count):
    even = [(i, i + 1) for i in range(0, count - 1, 2)]
    odd = [(i, i + 1) for i in range(1, count - 1, 2)]
    far_a = [(i, i + 2) for i in range(count - 2) if i % 4 in (0, 1)]
    far_b = [(i, i + 2) for i in range(count - 2) if i % 4 in (2, 3)]
    return [pairs + [(j, i) for i, j in pairs] for pairs in (even, odd, far_a, far_b)]


def swap(value, axis, pairs):
    return lax.ppermute(value, axis, pairs)


def bit_table(window_ref):
    bits = jnp.int32(0)
    for i in range(window_ref.shape[0]):
        code = (window_ref[i, 0] + 1) * 9 + (window_ref[i, 1] + 1) * 3 + (window_ref[i, 2] + 1)
        bits = bits | jnp.left_shift(jnp.int32(1), code)
    return bits


def position_facts(place_ref, frame_count, strip_count):
    frame = place_ref[0]
    strip = place_ref[1]
    step_f = 1 - 2 * (frame & 1)
    step_s = 1 - 2 * (strip & 1)
    return (
        frame,
        step_f,
        step_s,
        ((frame + step_f >= 0) & (frame + step_f < frame_count)).astype(jnp.int32),
        ((frame - step_f >= 0) & (frame - step_f < frame_count)).astype(jnp.int32),
        ((strip + step_s >= 0) & (strip + step_s < strip_count)).astype(jnp.int32),
        ((strip - step_s >= 0) & (strip - step_s < strip_count)).astype(jnp.int32),
    )


def fill_bias(bias_ref, slots, window_ref, place_ref, frame_count, strip_count, height, strip):
    bits = bit_table(window_ref)
    _, step_f, step_s, has_fa, has_fb, has_sa, has_sb = position_facts(
        place_ref, frame_count, strip_count
    )
    rows = height * strip
    half = height * TW
    tiles = strip // TW
    col_a = jnp.where(step_s > 0, tiles, -1)
    col_b = jnp.where(step_s > 0, -1, tiles)
    frames = ((0, 1), (-step_f, has_fa), (step_f, has_fb))
    for place, slot in enumerate(slots):
        off_time, has_f = frames[slot]
        start = 0
        for length, wide, k_col, has_s in (
            (rows, strip, None, 1),
            (half, TW, col_a, has_sa),
            (half, TW, col_b, has_sb),
        ):
            key_idx = lax.broadcasted_iota(jnp.int32, (length, rows), 0)
            query_idx = lax.broadcasted_iota(jnp.int32, (length, rows), 1)
            off_high = key_idx // (wide * TH) - query_idx // (strip * TH)
            k_wide = (key_idx % wide) // TW if k_col is None else k_col
            off_wide = k_wide - (query_idx % strip) // TW
            near = (jnp.abs(off_wide) <= 1) & (jnp.abs(off_high) <= 1)
            code = (off_time + 1) * 9 + (off_high + 1) * 3 + (off_wide + 1)
            listed = jnp.right_shift(bits, jnp.where(near, code, 0)) & 1
            flag = jnp.where(near, listed, 0) * (has_f * has_s)
            bias_ref[start : start + length, place * rows : (place + 1) * rows] = jnp.where(
                flag == 1, jnp.float32(0), jnp.float32(NEG)
            )
            start += length


def lanes_of(head):
    return slice(head * HD, (head + 1) * HD)


def head_rows(ref, head):
    return ref[0, :, :, lanes_of(head)].reshape(-1, HD)


def load_keys(own_ref, a_ref, b_ref, which, head):
    lanes = lanes_of(head)
    return jnp.concatenate(
        [head_rows(own_ref, head), a_ref[which, :, lanes], b_ref[which, :, lanes]], axis=0
    )


def dot_nt(a, b):
    return lax.dot_general(a, b, (((1,), (1,)), ((), ())), preferred_element_type=jnp.float32)


def run_copies(pairs, sems):
    copies = [pltpu.make_async_copy(src, dst, sems.at[i]) for i, (src, dst) in enumerate(pairs)]
    for copy in copies:
        copy.start()
    for copy in copies:
        copy.wait()


def stage_kernel(sizes, place_ref, k_in, v_in, k_out, v_out, a_out, b_out, sems):
    _, _, height, strip = sizes
    even = (place_ref[1] & 1) == 0
    start_a = pl.multiple_of(jnp.where(even, strip - TW, 0), TW)
    start_b = pl.multiple_of(jnp.where(even, 0, strip - TW), TW)
    pairs = []
    for edge, start in ((a_out, start_a), (b_out, start_b)):
        for which, ref in enumerate((k_in, v_in)):
            for row in range(height):
                pairs.append((ref.at[0, row, pl.ds(start, TW), :], edge.at[which, row * TW : (row + 1) * TW, :]))
    run_copies(pairs + [(k_in, k_out), (v_in, v_out)], sems)


def scores_kernel(sizes, window_ref, place_ref, q0, qa, qb, g0, k0, v0, ha, hb, expo_out, gp_out, st_out, delta_out, bias_ref):
    rows = sizes[2] * sizes[3]
    fill_bias(bias_ref, (0, 1, 2), window_ref, place_ref, *sizes)
    for head in range(st_out.shape[0]):
        key = load_keys(k0, ha, hb, 0, head)
        value = load_keys(v0, ha, hb, 1, head)
        query = jnp.concatenate([head_rows(r, head) for r in (q0, qa, qb)], axis=0)
        scores = dot_nt(key, query) * SCALE2 + bias_ref[...]
        grad_probs = dot_nt(value, head_rows(g0, head))
        top = jnp.max(scores, axis=0, keepdims=True)
        expo = jnp.exp2(scores - top)
        total = jnp.sum(expo, axis=0, keepdims=True)
        inverse = 1.0 / total
        expo_out[head] = expo
        gp_out[head] = grad_probs
        st_out[head] = jnp.concatenate([top + jnp.log2(total), top, inverse], axis=0)
        delta_out[head] = jnp.sum(expo[:, :rows] * grad_probs, axis=0, keepdims=True) * inverse[:, :rows]


def deltas_kernel(sizes, place_ref, ga, gb, v0, ha, hb, expo, st, own_delta, gp_out, delta_out, a_out, b_out, c_out, d_out):
    rows = sizes[2] * sizes[3]
    far_slot_a = ((place_ref[0] & 3) == 0) | ((place_ref[0] & 3) == 3)
    for head in range(st.shape[0]):
        value = load_keys(v0, ha, hb, 1, head)
        grad = jnp.concatenate([head_rows(ga, head), head_rows(gb, head)], axis=0)
        grad_probs = dot_nt(value, grad)
        gp_out[head] = grad_probs
        stat = st[head]
        near = jnp.sum(expo[head, :, rows:] * grad_probs, axis=0, keepdims=True) * stat[2:3, rows:]
        delta = jnp.concatenate([own_delta[head], near], axis=1)
        delta_out[head] = delta
        own, part_a, part_b = (
            jnp.concatenate([x[:, i * rows : (i + 1) * rows] for x in (stat[0:1], delta)], axis=0)
            for i in range(3)
        )
        a_out[head] = jnp.concatenate([own, part_a], axis=0)
        b_out[head] = jnp.concatenate([own, part_b], axis=0)
        c_out[head] = jnp.where(far_slot_a, part_a, part_b)
        d_out[head] = jnp.where(far_slot_a, part_b, part_a)


def merge(parts):
    top = parts[0][0]
    for lse, _ in parts[1:]:
        top = jnp.maximum(top, lse)
    weight_sum = jnp.zeros_like(top)
    delta_sum = jnp.zeros_like(top)
    for lse, delta in parts:
        weight = jnp.exp2(lse - top)
        weight_sum = weight_sum + weight
        delta_sum = delta_sum + weight * delta
    return jnp.maximum(top + jnp.log2(weight_sum), FLOOR), delta_sum / weight_sum


def halo_kernel(sizes, place_ref, q0, qa, qb, g0, ga, gb, expo, p0, pn, st, local_delta, a_st, b_st, c_st, d_st, rb_out, ra_out, row_out):
    frame_count, strip_count, height, strip = sizes
    rows = height * strip
    half = height * TW
    frame, step_f, _, has_fa, has_fb, _, _ = position_facts(place_ref, frame_count, strip_count)
    beyond_a = frame + 2 * step_f
    beyond_b = frame - 2 * step_f
    has_ba = (beyond_a >= 0) & (beyond_a < frame_count)
    has_bb = (beyond_b >= 0) & (beyond_b < frame_count)
    far_slot_a = ((frame & 3) == 0) | ((frame & 3) == 3)

    def part(block, row, exists):
        return (jnp.where(exists, block[row : row + 1, :], NEG), block[row + 1 : row + 2, :])

    for head in range(st.shape[0]):
        stat, local, from_a, from_b, from_c, from_d = (
            r[head] for r in (st, local_delta, a_st, b_st, c_st, d_st)
        )
        own, near_a, near_b = (
            (stat[0:1, i * rows : (i + 1) * rows], local[:, i * rows : (i + 1) * rows]) for i in range(3)
        )
        far_a = jnp.where(far_slot_a, from_c, from_d)
        far_b = jnp.where(far_slot_a, from_d, from_c)
        merged = [
            merge([own, part(from_a, 2, has_fa == 1), part(from_b, 2, has_fb == 1)]),
            merge([near_a, part(from_a, 0, has_fa == 1), part(far_a, 0, has_ba)]),
            merge([near_b, part(from_b, 0, has_fb == 1), part(far_b, 0, has_bb)]),
        ]
        lse = jnp.concatenate([m[0] for m in merged], axis=1)
        delta = jnp.concatenate([m[1] for m in merged], axis=1)
        row = jnp.concatenate([jnp.exp2(stat[1:2] - lse), delta], axis=0)
        row_out[head] = row
        key_part, value_part = head_grads(
            head, slice(rows, rows + 2 * half), row, q0, qa, qb, g0, ga, gb, expo, p0, pn
        )
        lanes = lanes_of(head)
        for out, lo in ((ra_out, 0), (rb_out, half)):
            out[0, :, lanes] = key_part[lo : lo + half].astype(jnp.bfloat16)
            out[1, :, lanes] = value_part[lo : lo + half].astype(jnp.bfloat16)


def head_grads(head, keys, row, q0, qa, qb, g0, ga, gb, expo_ref, p0, pn):
    query = jnp.concatenate([head_rows(r, head) for r in (q0, qa, qb)], axis=0)
    grad = jnp.concatenate([head_rows(r, head) for r in (g0, ga, gb)], axis=0)
    expo = expo_ref[head, keys, :]
    grad_probs = jnp.concatenate([p0[head, keys, :], pn[head, keys, :]], axis=1)
    factor = row[0:1]
    probs = expo * factor
    grad_scores = (expo * (factor * SCALE) * (grad_probs - row[1:2])).astype(jnp.bfloat16)
    value_part = jnp.dot(probs.astype(jnp.bfloat16), grad, preferred_element_type=jnp.float32)
    key_part = jnp.dot(grad_scores, query, preferred_element_type=jnp.float32)
    return key_part, value_part


def main_kernel(sizes, row_st, q0, qa, qb, g0, ga, gb, expo, p0, pn, dk_out, dv_out):
    rows = sizes[2] * sizes[3]
    for head in range(row_st.shape[0]):
        key_part, value_part = head_grads(
            head, slice(0, rows), row_st[head], q0, qa, qb, g0, ga, gb, expo, p0, pn
        )
        lanes = lanes_of(head)
        dk_out[:, lanes] = key_part
        dv_out[:, lanes] = value_part


def finish_kernel(sizes, place_ref, rb, ra, dk, dv, dk_out, dv_out, full_ref, sems):
    _, _, height, strip = sizes
    even = (place_ref[1] & 1) == 0
    count = height // FINISH_STEPS
    copies = []
    for step in range(FINISH_STEPS):
        lines = slice(step * count, (step + 1) * count)
        edge = slice(step * count * TW, (step + 1) * count * TW)
        span = slice(step * count * strip, (step + 1) * count * strip)
        for which, (part, out) in enumerate(((dk, dk_out), (dv, dv_out))):
            from_a = ra[which, edge, :].astype(jnp.float32).reshape(count, TW, -1)
            from_b = rb[which, edge, :].astype(jnp.float32).reshape(count, TW, -1)
            full = part[span, :].reshape(count, strip, -1)
            left = full[:, :TW] + jnp.where(even, from_b, from_a)
            right = full[:, TW:] + jnp.where(even, from_a, from_b)
            full_ref[which, lines] = jnp.concatenate([left, right], axis=1).astype(jnp.bfloat16)
            copy = pltpu.make_async_copy(
                full_ref.at[which, lines], out.at[0, lines], sems.at[2 * step + which]
            )
            copy.start()
            copies.append(copy)
    for copy in copies:
        copy.wait()


def vmem(value):
    return pltpu.with_memory_space_constraint(value, pltpu.VMEM)


def on_device(queries, keys, values, grad_out, window):
    _, height, strip, chans = queries.shape
    heads = chans // HD
    rows = height * strip
    half = height * TW
    ext = rows + 2 * half
    frame_count = lax.axis_size("frame")
    strip_count = lax.axis_size("tile")
    sizes = (frame_count, strip_count, height, strip)
    frame_even, frame_odd, far_c, far_d = pair_lists(frame_count)
    tile_even, tile_odd, _, _ = pair_lists(strip_count)
    frame_pos = lax.axis_index("frame")
    strip_pos = lax.axis_index("tile")
    place = jnp.stack([frame_pos, strip_pos]).astype(jnp.int32)

    qa = swap(queries, "frame", frame_even)
    qb = swap(queries, "frame", frame_odd)
    ga = swap(grad_out, "frame", frame_even)
    gb = swap(grad_out, "frame", frame_odd)

    raw = pl.BlockSpec(memory_space=pl.ANY)
    smem = pl.BlockSpec(memory_space=pltpu.SMEM)
    whole = pl.BlockSpec(memory_space=pltpu.VMEM)

    def call(kernel, name, scalars, arrays, outs, scratch=(), flops=0):
        return pl.pallas_call(
            lambda *refs: kernel(sizes, *refs),
            name=name,
            in_specs=[smem] * len(scalars) + [whole] * len(arrays),
            out_specs=[whole] * len(outs),
            out_shape=[pltpu.VMEM(shape, dtype) for shape, dtype in outs],
            scratch_shapes=list(scratch),
            cost_estimate=pl.CostEstimate(flops=flops, transcendentals=0, bytes_accessed=0),
            compiler_params=pltpu.CompilerParams(vmem_limit_bytes=KERNEL_VMEM),
        )(*scalars, *[vmem(x) for x in arrays])

    f32 = jnp.float32
    edge = (2, half, chans)
    keys, values, ea, eb = pl.pallas_call(
        lambda *refs: stage_kernel(sizes, *refs),
        name="stage",
        in_specs=[smem, raw, raw],
        out_specs=[whole] * 4,
        out_shape=[pltpu.VMEM(shape, jnp.bfloat16) for shape in (keys.shape, values.shape, edge, edge)],
        scratch_shapes=[pltpu.SemaphoreType.DMA((4 * height + 2,))],
        compiler_params=pltpu.CompilerParams(vmem_limit_bytes=KERNEL_VMEM),
        cost_estimate=pl.CostEstimate(flops=0, transcendentals=0, bytes_accessed=0),
    )(place, *[pltpu.with_memory_space_constraint(x, pltpu.HBM) for x in (keys, values)])
    ha = swap(ea, "tile", tile_even)
    hb = swap(eb, "tile", tile_odd)
    expo, p0, st, own_delta = call(
        scores_kernel,
        "scores",
        (window, place),
        (queries, qa, qb, grad_out, keys, values, ha, hb),
        [
            ((heads, ext, 3 * rows), f32),
            ((heads, ext, rows), f32),
            ((heads, 3, 3 * rows), f32),
            ((heads, 1, rows), f32),
        ],
        [pltpu.VMEM((ext, 3 * rows), f32)],
    )
    pn, local_delta, a_st, b_st, c_st, d_st = call(
        deltas_kernel,
        "deltas",
        (place,),
        (ga, gb, values, ha, hb, expo, st, own_delta),
        [((heads, ext, 2 * rows), f32), ((heads, 1, 3 * rows), f32)]
        + [((heads, n, rows), f32) for n in (4, 4, 2, 2)],
    )
    a_st = swap(a_st, "frame", frame_even)
    b_st = swap(b_st, "frame", frame_odd)
    if far_c:
        c_st = swap(c_st, "frame", far_c)
    if far_d:
        d_st = swap(d_st, "frame", far_d)

    data = (queries, qa, qb, grad_out, ga, gb, expo, p0, pn)
    rb, ra, row = call(
        halo_kernel,
        "halo_grads",
        (place,),
        data + (st, local_delta, a_st, b_st, c_st, d_st),
        [((2, half, chans), jnp.bfloat16)] * 2 + [((heads, 2, 3 * rows), f32)],
    )
    rb = swap(rb, "tile", tile_odd)
    ra = swap(ra, "tile", tile_even)
    dk, dv = call(
        main_kernel,
        "main_grads",
        (),
        (row,) + data,
        [((rows, chans), f32)] * 2,
        flops=FLOPS,
    )

    return pl.pallas_call(
        lambda *refs: finish_kernel(sizes, *refs),
        name="finish",
        compiler_params=pltpu.CompilerParams(vmem_limit_bytes=KERNEL_VMEM),
        in_specs=[smem] + [whole] * 4,
        out_specs=[raw, raw],
        out_shape=[jax.ShapeDtypeStruct(queries.shape, jnp.bfloat16)] * 2,
        scratch_shapes=[
            pltpu.VMEM((2, height, strip, chans), jnp.bfloat16),
            pltpu.SemaphoreType.DMA((2 * FINISH_STEPS,)),
        ],
    )(place, vmem(rb), vmem(ra), vmem(dk), vmem(dv))


def solution(mesh):
    spec = P(("clip", "frame"), None, "tile", None)
    return jax.shard_map(
        on_device,
        mesh=mesh,
        in_specs=(spec, spec, spec, spec, P()),
        out_specs=(spec, spec),
        check_vma=False,
    )
```

```python
import math

import jax
import jax.numpy as jnp
from jax import lax
from jax.experimental import pallas as pl
from jax.experimental.pallas import tpu as pltpu
from jax.sharding import PartitionSpec as P

HD = 128
TH = 4
TW = 8
FINISH_STEPS = 4
FLOPS = 1_500_000_000
KERNEL_VMEM = 16 << 20
NEG = -1e30
FLOOR = -1e29
SCALE = HD ** (-0.5)
SCALE2 = SCALE * math.log2(math.e)


def pair_lists(count):
    even = [(i, i + 1) for i in range(0, count - 1, 2)]
    odd = [(i, i + 1) for i in range(1, count - 1, 2)]
    far_a = [(i, i + 2) for i in range(count - 2) if i % 4 in (0, 1)]
    far_b = [(i, i + 2) for i in range(count - 2) if i % 4 in (2, 3)]
    return [pairs + [(j, i) for i, j in pairs] for pairs in (even, odd, far_a, far_b)]


def swap(value, axis, pairs):
    return lax.ppermute(value, axis, pairs)


def bit_table(window_ref):
    bits = jnp.int32(0)
    for i in range(window_ref.shape[0]):
        code = (window_ref[i, 0] + 1) * 9 + (window_ref[i, 1] + 1) * 3 + (window_ref[i, 2] + 1)
        bits = bits | jnp.left_shift(jnp.int32(1), code)
    return bits


def position_facts(place_ref, frame_count, strip_count):
    frame = place_ref[0]
    strip = place_ref[1]
    step_f = 1 - 2 * (frame & 1)
    step_s = 1 - 2 * (strip & 1)
    return (
        frame,
        step_f,
        step_s,
        ((frame + step_f >= 0) & (frame + step_f < frame_count)).astype(jnp.int32),
        ((frame - step_f >= 0) & (frame - step_f < frame_count)).astype(jnp.int32),
        ((strip + step_s >= 0) & (strip + step_s < strip_count)).astype(jnp.int32),
        ((strip - step_s >= 0) & (strip - step_s < strip_count)).astype(jnp.int32),
    )


def fill_bias(bias_ref, slots, window_ref, place_ref, frame_count, strip_count, height, strip):
    bits = bit_table(window_ref)
    _, step_f, step_s, has_fa, has_fb, has_sa, has_sb = position_facts(
        place_ref, frame_count, strip_count
    )
    rows = height * strip
    half = height * TW
    tiles = strip // TW
    col_a = jnp.where(step_s > 0, tiles, -1)
    col_b = jnp.where(step_s > 0, -1, tiles)
    frames = ((0, 1), (-step_f, has_fa), (step_f, has_fb))
    for place, slot in enumerate(slots):
        off_time, has_f = frames[slot]
        start = 0
        for length, wide, k_col, has_s in (
            (rows, strip, None, 1),
            (half, TW, col_a, has_sa),
            (half, TW, col_b, has_sb),
        ):
            key_idx = lax.broadcasted_iota(jnp.int32, (length, rows), 0)
            query_idx = lax.broadcasted_iota(jnp.int32, (length, rows), 1)
            off_high = key_idx // (wide * TH) - query_idx // (strip * TH)
            k_wide = (key_idx % wide) // TW if k_col is None else k_col
            off_wide = k_wide - (query_idx % strip) // TW
            near = (jnp.abs(off_wide) <= 1) & (jnp.abs(off_high) <= 1)
            code = (off_time + 1) * 9 + (off_high + 1) * 3 + (off_wide + 1)
            listed = jnp.right_shift(bits, jnp.where(near, code, 0)) & 1
            flag = jnp.where(near, listed, 0) * (has_f * has_s)
            bias_ref[start : start + length, place * rows : (place + 1) * rows] = jnp.where(
                flag == 1, jnp.float32(0), jnp.float32(NEG)
            )
            start += length


def lanes_of(head):
    return slice(head * HD, (head + 1) * HD)


def head_rows(ref, head):
    return ref[0, :, :, lanes_of(head)].reshape(-1, HD)


def load_keys(own_ref, a_ref, b_ref, which, head):
    lanes = lanes_of(head)
    return jnp.concatenate(
        [head_rows(own_ref, head), a_ref[which, :, lanes], b_ref[which, :, lanes]], axis=0
    )


def dot_nt(a, b):
    return lax.dot_general(a, b, (((1,), (1,)), ((), ())), preferred_element_type=jnp.float32)


def run_copies(pairs, sems):
    copies = [pltpu.make_async_copy(src, dst, sems.at[i]) for i, (src, dst) in enumerate(pairs)]
    for copy in copies:
        copy.start()
    for copy in copies:
        copy.wait()


def stage_kernel(sizes, place_ref, _, k_in, v_in, k_out, v_out, a_out, b_out, sems):
    _, _, height, strip = sizes
    even = (place_ref[1] & 1) == 0
    start_a = pl.multiple_of(jnp.where(even, strip - TW, 0), TW)
    start_b = pl.multiple_of(jnp.where(even, 0, strip - TW), TW)
    pairs = []
    for edge, start in ((a_out, start_a), (b_out, start_b)):
        for which, ref in enumerate((k_in, v_in)):
            for row in range(height):
                pairs.append((ref.at[0, row, pl.ds(start, TW), :], edge.at[which, row * TW : (row + 1) * TW, :]))
    run_copies(pairs + [(k_in, k_out), (v_in, v_out)], sems)


def scores_kernel(sizes, window_ref, place_ref, q0, qa, qb, g0, k0, v0, ha, hb, expo_out, gp_out, st_out, delta_out, bias_ref):
    rows = sizes[2] * sizes[3]
    fill_bias(bias_ref, (0, 1, 2), window_ref, place_ref, *sizes)
    for head in range(st_out.shape[0]):
        key = load_keys(k0, ha, hb, 0, head)
        value = load_keys(v0, ha, hb, 1, head)
        query = jnp.concatenate([head_rows(r, head) for r in (q0, qa, qb)], axis=0)
        scores = dot_nt(key, query) * SCALE2 + bias_ref[...]
        grad_probs = dot_nt(value, head_rows(g0, head))
        top = jnp.max(scores, axis=0, keepdims=True)
        expo = jnp.exp2(scores - top)
        total = jnp.sum(expo, axis=0, keepdims=True)
        inverse = 1.0 / total
        expo_out[head] = expo
        gp_out[head] = grad_probs
        st_out[head] = jnp.concatenate([top + jnp.log2(total), top, inverse], axis=0)
        delta_out[head] = jnp.sum(expo[:, :rows] * grad_probs, axis=0, keepdims=True) * inverse[:, :rows]


def deltas_kernel(sizes, place_ref, ga, gb, v0, ha, hb, expo, st, own_delta, gp_out, delta_out, a_out, b_out, c_out, d_out):
    rows = sizes[2] * sizes[3]
    far_slot_a = ((place_ref[0] & 3) == 0) | ((place_ref[0] & 3) == 3)
    for head in range(st.shape[0]):
        value = load_keys(v0, ha, hb, 1, head)
        grad = jnp.concatenate([head_rows(ga, head), head_rows(gb, head)], axis=0)
        grad_probs = dot_nt(value, grad)
        gp_out[head] = grad_probs
        stat = st[head]
        near = jnp.sum(expo[head, :, rows:] * grad_probs, axis=0, keepdims=True) * stat[2:3, rows:]
        delta = jnp.concatenate([own_delta[head], near], axis=1)
        delta_out[head] = delta
        own, part_a, part_b = (
            jnp.concatenate([x[:, i * rows : (i + 1) * rows] for x in (stat[0:1], delta)], axis=0)
            for i in range(3)
        )
        a_out[head] = jnp.concatenate([own, part_a], axis=0)
        b_out[head] = jnp.concatenate([own, part_b], axis=0)
        c_out[head] = jnp.where(far_slot_a, part_a, part_b)
        d_out[head] = jnp.where(far_slot_a, part_b, part_a)


def merge(parts):
    top = parts[0][0]
    for lse, _ in parts[1:]:
        top = jnp.maximum(top, lse)
    weight_sum = jnp.zeros_like(top)
    delta_sum = jnp.zeros_like(top)
    for lse, delta in parts:
        weight = jnp.exp2(lse - top)
        weight_sum = weight_sum + weight
        delta_sum = delta_sum + weight * delta
    return jnp.maximum(top + jnp.log2(weight_sum), FLOOR), delta_sum / weight_sum


def halo_kernel(sizes, place_ref, q0, qa, qb, g0, ga, gb, expo, p0, pn, st, local_delta, a_st, b_st, c_st, d_st, rb_out, ra_out, row_out):
    frame_count, strip_count, height, strip = sizes
    rows = height * strip
    half = height * TW
    frame, step_f, _, has_fa, has_fb, _, _ = position_facts(place_ref, frame_count, strip_count)
    beyond_a = frame + 2 * step_f
    beyond_b = frame - 2 * step_f
    has_ba = (beyond_a >= 0) & (beyond_a < frame_count)
    has_bb = (beyond_b >= 0) & (beyond_b < frame_count)
    far_slot_a = ((frame & 3) == 0) | ((frame & 3) == 3)

    def part(block, row, exists):
        return (jnp.where(exists, block[row : row + 1, :], NEG), block[row + 1 : row + 2, :])

    for head in range(st.shape[0]):
        stat, local, from_a, from_b, from_c, from_d = (
            r[head] for r in (st, local_delta, a_st, b_st, c_st, d_st)
        )
        own, near_a, near_b = (
            (stat[0:1, i * rows : (i + 1) * rows], local[:, i * rows : (i + 1) * rows]) for i in range(3)
        )
        far_a = jnp.where(far_slot_a, from_c, from_d)
        far_b = jnp.where(far_slot_a, from_d, from_c)
        merged = [
            merge([own, part(from_a, 2, has_fa == 1), part(from_b, 2, has_fb == 1)]),
            merge([near_a, part(from_a, 0, has_fa == 1), part(far_a, 0, has_ba)]),
            merge([near_b, part(from_b, 0, has_fb == 1), part(far_b, 0, has_bb)]),
        ]
        lse = jnp.concatenate([m[0] for m in merged], axis=1)
        delta = jnp.concatenate([m[1] for m in merged], axis=1)
        row = jnp.concatenate([jnp.exp2(stat[1:2] - lse), delta], axis=0)
        row_out[head] = row
        key_part, value_part = head_grads(
            head, slice(rows, rows + 2 * half), row, q0, qa, qb, g0, ga, gb, expo, p0, pn
        )
        lanes = lanes_of(head)
        for out, lo in ((ra_out, 0), (rb_out, half)):
            out[0, :, lanes] = key_part[lo : lo + half].astype(jnp.bfloat16)
            out[1, :, lanes] = value_part[lo : lo + half].astype(jnp.bfloat16)


def head_grads(head, keys, row, q0, qa, qb, g0, ga, gb, expo_ref, p0, pn):
    query = jnp.concatenate([head_rows(r, head) for r in (q0, qa, qb)], axis=0)
    grad = jnp.concatenate([head_rows(r, head) for r in (g0, ga, gb)], axis=0)
    expo = expo_ref[head, keys, :]
    grad_probs = jnp.concatenate([p0[head, keys, :], pn[head, keys, :]], axis=1)
    factor = row[0:1]
    probs = expo * factor
    grad_scores = (expo * (factor * SCALE) * (grad_probs - row[1:2])).astype(jnp.bfloat16)
    value_part = jnp.dot(probs.astype(jnp.bfloat16), grad, preferred_element_type=jnp.float32)
    key_part = jnp.dot(grad_scores, query, preferred_element_type=jnp.float32)
    return key_part, value_part


def main_kernel(sizes, row_st, q0, qa, qb, g0, ga, gb, expo, p0, pn, dk_out, dv_out):
    rows = sizes[2] * sizes[3]
    for head in range(row_st.shape[0]):
        key_part, value_part = head_grads(
            head, slice(0, rows), row_st[head], q0, qa, qb, g0, ga, gb, expo, p0, pn
        )
        lanes = lanes_of(head)
        dk_out[:, lanes] = key_part
        dv_out[:, lanes] = value_part


def finish_kernel(sizes, place_ref, rb, ra, dk, dv, dk_out, dv_out, full_ref, sems):
    _, _, height, strip = sizes
    even = (place_ref[1] & 1) == 0
    count = height // FINISH_STEPS
    copies = []
    for step in range(FINISH_STEPS):
        lines = slice(step * count, (step + 1) * count)
        edge = slice(step * count * TW, (step + 1) * count * TW)
        span = slice(step * count * strip, (step + 1) * count * strip)
        for which, (part, out) in enumerate(((dk, dk_out), (dv, dv_out))):
            from_a = ra[which, edge, :].astype(jnp.float32).reshape(count, TW, -1)
            from_b = rb[which, edge, :].astype(jnp.float32).reshape(count, TW, -1)
            full = part[span, :].reshape(count, strip, -1)
            left = full[:, :TW] + jnp.where(even, from_b, from_a)
            right = full[:, TW:] + jnp.where(even, from_a, from_b)
            full_ref[which, lines] = jnp.concatenate([left, right], axis=1).astype(jnp.bfloat16)
            copy = pltpu.make_async_copy(
                full_ref.at[which, lines], out.at[0, lines], sems.at[2 * step + which]
            )
            copy.start()
            copies.append(copy)
    for copy in copies:
        copy.wait()


def vmem(value):
    return pltpu.with_memory_space_constraint(value, pltpu.VMEM)


def on_device(queries, keys, values, grad_out, window):
    _, height, strip, chans = queries.shape
    heads = chans // HD
    rows = height * strip
    half = height * TW
    ext = rows + 2 * half
    frame_count = lax.axis_size("frame")
    strip_count = lax.axis_size("tile")
    sizes = (frame_count, strip_count, height, strip)
    frame_even, frame_odd, far_c, far_d = pair_lists(frame_count)
    tile_even, tile_odd, _, _ = pair_lists(strip_count)
    frame_pos = lax.axis_index("frame")
    strip_pos = lax.axis_index("tile")
    place = jnp.stack([frame_pos, strip_pos]).astype(jnp.int32)

    qa = swap(queries, "frame", frame_even)
    qb = swap(queries, "frame", frame_odd)
    ga = swap(grad_out, "frame", frame_even)
    gb = swap(grad_out, "frame", frame_odd)

    raw = pl.BlockSpec(memory_space=pl.ANY)
    smem = pl.BlockSpec(memory_space=pltpu.SMEM)
    whole = pl.BlockSpec(memory_space=pltpu.VMEM)

    def call(kernel, name, scalars, arrays, outs, scratch=(), flops=0):
        return pl.pallas_call(
            lambda *refs: kernel(sizes, *refs),
            name=name,
            in_specs=[smem] * len(scalars) + [whole] * len(arrays),
            out_specs=[whole] * len(outs),
            out_shape=[pltpu.VMEM(shape, dtype) for shape, dtype in outs],
            scratch_shapes=list(scratch),
            cost_estimate=pl.CostEstimate(flops=flops, transcendentals=0, bytes_accessed=0),
            compiler_params=pltpu.CompilerParams(vmem_limit_bytes=KERNEL_VMEM),
        )(*scalars, *[vmem(x) for x in arrays])

    f32 = jnp.float32
    edge = (2, half, chans)
    keys, values, ea, eb = pl.pallas_call(
        lambda *refs: stage_kernel(sizes, *refs),
        name="stage",
        in_specs=[smem, whole, raw, raw],
        out_specs=[whole] * 4,
        out_shape=[pltpu.VMEM(shape, jnp.bfloat16) for shape in (keys.shape, values.shape, edge, edge)],
        scratch_shapes=[pltpu.SemaphoreType.DMA((4 * height + 2,))],
        compiler_params=pltpu.CompilerParams(vmem_limit_bytes=KERNEL_VMEM),
        cost_estimate=pl.CostEstimate(flops=0, transcendentals=0, bytes_accessed=0),
    )(place, vmem(ga), *[pltpu.with_memory_space_constraint(x, pltpu.HBM) for x in (keys, values)])
    ha = swap(ea, "tile", tile_even)
    hb = swap(eb, "tile", tile_odd)
    expo, p0, st, own_delta = call(
        scores_kernel,
        "scores",
        (window, place),
        (queries, qa, qb, grad_out, keys, values, ha, hb),
        [
            ((heads, ext, 3 * rows), f32),
            ((heads, ext, rows), f32),
            ((heads, 3, 3 * rows), f32),
            ((heads, 1, rows), f32),
        ],
        [pltpu.VMEM((ext, 3 * rows), f32)],
    )
    pn, local_delta, a_st, b_st, c_st, d_st = call(
        deltas_kernel,
        "deltas",
        (place,),
        (ga, gb, values, ha, hb, expo, st, own_delta),
        [((heads, ext, 2 * rows), f32), ((heads, 1, 3 * rows), f32)]
        + [((heads, n, rows), f32) for n in (4, 4, 2, 2)],
    )
    a_st = swap(a_st, "frame", frame_even)
    b_st = swap(b_st, "frame", frame_odd)
    if far_c:
        c_st = swap(c_st, "frame", far_c)
    if far_d:
        d_st = swap(d_st, "frame", far_d)

    data = (queries, qa, qb, grad_out, ga, gb, expo, p0, pn)
    rb, ra, row = call(
        halo_kernel,
        "halo_grads",
        (place,),
        data + (st, local_delta, a_st, b_st, c_st, d_st),
        [((2, half, chans), jnp.bfloat16)] * 2 + [((heads, 2, 3 * rows), f32)],
    )
    rb = swap(rb, "tile", tile_odd)
    ra = swap(ra, "tile", tile_even)
    dk, dv = call(
        main_kernel,
        "main_grads",
        (),
        (row,) + data,
        [((rows, chans), f32)] * 2,
        flops=FLOPS,
    )

    return pl.pallas_call(
        lambda *refs: finish_kernel(sizes, *refs),
        name="finish",
        compiler_params=pltpu.CompilerParams(vmem_limit_bytes=KERNEL_VMEM),
        in_specs=[smem] + [whole] * 4,
        out_specs=[raw, raw],
        out_shape=[jax.ShapeDtypeStruct(queries.shape, jnp.bfloat16)] * 2,
        scratch_shapes=[
            pltpu.VMEM((2, height, strip, chans), jnp.bfloat16),
            pltpu.SemaphoreType.DMA((2 * FINISH_STEPS,)),
        ],
    )(place, vmem(rb), vmem(ra), vmem(dk), vmem(dv))


def solution(mesh):
    spec = P(("clip", "frame"), None, "tile", None)
    return jax.shard_map(
        on_device,
        mesh=mesh,
        in_specs=(spec, spec, spec, spec, P()),
        out_specs=(spec, spec),
        check_vma=False,
    )
```
